32 devices in a mesh: atom: 8 (over z, x), aux: 4 (over y, core).
Axes of the slice: x: 2, y: 2, z: 4, core: 2. Of those that a mesh axis runs over, the one named last changes fastest.
Arguments:
- three_index: bfloat16 [128, 32, 128, 128], P('atom', 'aux'), may hold values from -6 to 6
- pair_mask: int32 [128, 8, 8], P('atom'), may hold values 0 or 1
- pair_owner: int32 [128, 1], P('atom'), may hold values from 0 to 7; in each aligned block of 16 rows (0 to 15, 16 to 31, ...) at most 2 rows name the same one
- pair_sub: int32 [128], P('atom'), may hold values from 0 to 3
- pair_nu: int32 [128], P('atom'), may hold values from 0 to 31
- live_count: int32 [8], P('atom'), may hold values from 1 to 16, 96 in all
- coefficients: bfloat16 [4096, 128], P('atom'), may hold values from -0.5 to 0.5
- fit_matrix: bfloat16 [32, 32], P('aux'), as said below
Outputs:
- exchange: float32 [4096, 4096], P('atom', 'aux')
The draws below stay inside these ranges and needn't reach their ends.
Inputs may be any that keep to these rules, and one draw needn't show every extreme that they name: `pair_owner`: among the 16 slots of one atom index, at most 2 name the same owner, and in every draw some owner is named exactly 2 times by some atom index's slots. The first live_count[a] slots of atom index a are live; some atom index has all 16 slots live. `fit_matrix`: Symmetric.
All inputs are finite; a program needn't handle non-finite values. No bound on the sum of `pair_mask` or of `live_count` on one device may be relied on, other than what follows from the above.
Results may differ from the reference program's by a relative error of at most 0.012.
Values may be sent and summed in bfloat16 or wider, within the bound.
A program may use at most 128 MiB of HBM per device.

```python
import math
import jax
import jax.numpy as jnp
import numpy as np
from jax import lax

BLK = 128
AB = 8
NOCC = 128
AUX_DEV = 8
MB_DEV = 4
TASK_DEV = 16
CAP = 2
NAUX = 32
NB = 32
NBF = 4096
PAIRS = 128
N_ATOM = 8
N_AUX = 4


def draw_fit_matrix(key, part):
    first_key, second_key = jax.random.split(jax.random.fold_in(key, 17), 2)
    base = jax.random.normal(first_key, (NAUX, NAUX), jnp.float32) * NAUX ** (-0.5)
    matrix = (base + base.T) * 0.7071
    diagonal = jax.random.uniform(second_key, (NAUX,), jnp.float32, -0.5, 0.5)
    matrix = matrix + jnp.diag(diagonal)
    return matrix.astype(jnp.bfloat16)


def with_ends(result, own_key, low, largest):
    longest = result.shape.index(max(result.shape))
    spots = []
    for shift in (0, 1):
        where = [jax.random.randint(jax.random.fold_in(own_key, axis), (), 0, length) for axis, length in enumerate(result.shape)]
        where[longest] = (where[longest] + shift) % result.shape[longest]
        spots.append(tuple(where))
    return result.at[spots[0]].set(low).at[spots[1]].set(largest)


def shard_levels(own_key, shape, cuts, least, largest):
    factor_of, own = 1.0, jax.random.fold_in(own_key, 6)
    for dim, parts in cuts:
        heights = jnp.exp(jax.random.uniform(jax.random.fold_in(own, dim), (parts,), jnp.float32, least / len(cuts), largest / len(cuts)))
        factor_of = factor_of * jnp.repeat(heights, shape[dim] // parts).reshape([-1 if axis == dim else 1 for axis in range(len(shape))])
    return factor_of


def profile(amount, total, limit, lean):
    weights = [(1 << 20) // math.isqrt(rank ** lean) + 1 for rank in range(2, amount + 1)]
    surplus, holding = total - limit - (amount - 1), [1] * (amount - 1)
    while surplus > 0:
        candidates = [i for i in range(amount - 1) if holding[i] < limit]
        mass, remaining = sum([weights[i] for i in candidates]), surplus
        for i in candidates:
            more = min(limit - holding[i], max(1, remaining * weights[i] // mass), surplus)
            holding[i] = holding[i] + more
            surplus = surplus - more
    return np.array([limit] + holding)


def ragged(key, count, total, limit, skew):
    if count == 2:
        one = jax.random.randint(key, (), max(1, total - limit), min(limit, total - 1) + 1)
        return jnp.stack([one, total - one])
    lengths = jnp.asarray(profile(count, total, limit, skew), jnp.int32)
    couples = (count - 1) // 2
    donor, sink = lengths[1:1 + 2 * couples:2], lengths[2:2 + 2 * couples:2]
    slack = jnp.minimum(donor - 1, limit - sink)
    passed = jax.random.randint(jax.random.fold_in(key, 1), (couples,), 0, 1 << 20) % (slack + 1)
    lengths = lengths.at[1:1 + 2 * couples:2].set(donor - passed).at[2:2 + 2 * couples:2].set(sink + passed)
    return lengths[jax.random.permutation(jax.random.fold_in(key, 2), count)]


def shared_out(rng, own, number, rows, amount, top, limit, skew):
    ranking = jax.random.permutation(rng, amount)
    heavy_load, usual = load_shares(amount, rows * top, limit, skew, True), load_shares(amount, rows * top, limit, skew, False)
    places = jnp.arange(amount)

    def named(lengths, turn):
        used = int((lengths > 0).sum())
        fixed = max(1, used // 4)
        moved = fixed + (places - fixed + turn * (used - fixed)) % max(1, amount - fixed)
        return jnp.zeros((amount,), jnp.int32).at[ranking[jnp.where(places < fixed, places, moved)]].set(jnp.asarray(lengths, jnp.int32))

    lengths = jnp.where(number % 4 == 0, named(heavy_load, number // 4), named(usual, number - number // 4 - 1))
    mixed = jax.random.permutation(jax.random.fold_in(own, 3), amount)
    source_of, receiver = mixed[0:amount // 2 * 2:2], mixed[1:amount // 2 * 2:2]
    margin = jnp.minimum(lengths[source_of] - 1, limit - lengths[receiver]) // 2
    margin = jnp.where((source_of == ranking[0]) | (receiver == ranking[0]) | (lengths[receiver] == 0), 0, jnp.maximum(margin, 0))
    moved = jax.random.randint(jax.random.fold_in(own, 4), (amount // 2,), 0, 1 << 20) % (margin + 1)
    lengths = lengths.at[source_of].add(-moved).at[receiver].add(moved)
    labels = jnp.searchsorted(jnp.cumsum(lengths), jnp.arange(rows * top), side="right").astype(jnp.int32)
    listing = labels.reshape(top, rows).T
    listing = listing[jax.random.permutation(jax.random.fold_in(own, 1), rows)]
    turn = jax.random.randint(jax.random.fold_in(own, 2), (rows, 1), 0, top)
    return jnp.take_along_axis(listing, (jnp.arange(top)[None, :] + turn) % top, axis=1)


def load_shares(number_of, total, limit, lean, full):
    loads = [(1 << 20) // math.isqrt(standing ** lean) + 1 for standing in range(1, number_of + 1)]
    largest = limit if full else min(limit, max(-(-total // number_of), total * loads[0] // sum(loads)))
    least = 1 if total - largest >= number_of - 1 else 0
    holding, surplus = [largest] + [least] * (number_of - 1), total - largest - least * (number_of - 1)
    while surplus > 0:
        candidates = [i for i in range(1, number_of) if holding[i] < largest] or [i for i in range(1, number_of) if holding[i] < limit]
        mass, remaining = sum([loads[i] for i in candidates]), surplus
        for i in candidates:
            more = min(limit - holding[i], max(1, remaining * loads[i] // mass), surplus)
            holding[i] = holding[i] + more
            surplus = surplus - more
    return np.array(holding)


def gaussian(stream_key, dims, spread, reach, cuts=(), kind=jnp.bfloat16):
    loudness = shard_levels(stream_key, dims, cuts, -0.22, 0.18) if cuts else 1.0
    drawn = jax.random.normal(stream_key, dims, jnp.float32) * spread * loudness
    return jnp.minimum(jnp.maximum(drawn, -reach), reach).astype(kind)


def setup_inputs(seed: int = 0) -> dict:
    key_of = jax.random.split(jax.random.key(seed), 9)
    three_index = gaussian(key_of[0], (PAIRS, NAUX, BLK, BLK), 1.0, 6.0, ((0, 8), (1, 4)))
    pair_mask = with_ends((jax.random.randint(key_of[1], (PAIRS, AB, AB), 0, 4) < 3).astype(jnp.int32), jax.random.fold_in(key_of[1], 1), 0, 1)
    pair_owner_keys = jax.random.split(jax.random.fold_in(key_of[2], 1), PAIRS // TASK_DEV)
    pair_owner_turns = jax.random.permutation(jax.random.fold_in(key_of[2], 3), PAIRS // TASK_DEV)
    pair_owner = jax.vmap(lambda own, number: shared_out(jax.random.fold_in(key_of[2], 2), own, number, TASK_DEV, N_ATOM, 1, CAP, 2))(pair_owner_keys, pair_owner_turns).reshape((PAIRS, 1))
    pair_sub = with_ends(jax.random.randint(key_of[3], (PAIRS,), 0, MB_DEV), jax.random.fold_in(key_of[3], 1), 0, MB_DEV - 1).astype(jnp.int32)
    pair_nu = with_ends(jax.random.randint(key_of[4], (PAIRS,), 0, NB), jax.random.fold_in(key_of[4], 1), 0, NB - 1).astype(jnp.int32)
    live_count = ragged(key_of[5], N_ATOM, N_ATOM * TASK_DEV * 3 // 4, TASK_DEV, 2).astype(jnp.int32)
    coefficients = gaussian(key_of[6], (NBF, NOCC), BLK ** -0.5, 0.5, ((0, 8),))
    fit_matrix = draw_fit_matrix(jax.random.fold_in(key_of[8], 71), 0)
    return {"three_index": three_index, "pair_mask": pair_mask, "pair_owner": pair_owner, "pair_sub": pair_sub, "pair_nu": pair_nu, "live_count": live_count, "coefficients": coefficients, "fit_matrix": fit_matrix}


def reference(three_index, pair_mask, pair_owner, pair_sub, pair_nu, live_count, coefficients, fit_matrix):
    block_size = three_index.shape[2]
    aux_total = fit_matrix.shape[0]
    basis_total = coefficients.shape[0]
    occupied = coefficients.shape[1]
    shell_size = block_size // pair_mask.shape[1]
    slot_index = jnp.arange(three_index.shape[0], dtype=jnp.int32)
    alive_mask = (slot_index % TASK_DEV) < live_count[slot_index // TASK_DEV]
    mu_blocks = (pair_owner[:, 0] * MB_DEV + pair_sub).astype(jnp.int32)
    zero_index = jnp.zeros((), jnp.int32)

    def add_pair(summed, inputs):
        tile_data, small_mask, nu_block, mu_block, alive_flag = inputs
        expanded = jnp.repeat(jnp.repeat(small_mask, shell_size, 0), shell_size, 1).astype(jnp.float32)
        masked = tile_data.astype(jnp.float32) * expanded
        orbital_rows = lax.dynamic_slice(coefficients, ((nu_block * block_size).astype(jnp.int32), zero_index), (block_size, occupied)).astype(jnp.float32)
        halfway = jnp.einsum("pmn,ni->pmi", masked, orbital_rows)
        rounded = lax.optimization_barrier(halfway.astype(jnp.bfloat16)).astype(jnp.float32)
        rounded = jnp.where(alive_flag, rounded, 0.0)
        start_row = (mu_block * block_size).astype(jnp.int32)
        current = lax.dynamic_slice(summed, (zero_index, start_row, zero_index), (aux_total, block_size, occupied))
        return lax.dynamic_update_slice(summed, current + rounded, (zero_index, start_row, zero_index)), None

    summed, _ = lax.scan(add_pair, jnp.zeros((aux_total, basis_total, occupied), jnp.float32), (three_index, pair_mask, pair_nu, mu_blocks, alive_mask))
    half_transformed = summed.astype(jnp.bfloat16)
    flat_input = lax.optimization_barrier(half_transformed).astype(jnp.float32).reshape(aux_total, basis_total * occupied)
    fitted = jnp.dot(fit_matrix.astype(jnp.float32), flat_input).astype(jnp.bfloat16)
    left_all = half_transformed.reshape(N_AUX, AUX_DEV, basis_total, occupied)
    right_all = fitted.reshape(N_AUX, AUX_DEV, basis_total, occupied)

    def add_share(summed_exchange, pieces):
        left_piece, right_piece = pieces
        left_rows = lax.optimization_barrier(left_piece).astype(jnp.float32).transpose(1, 0, 2).reshape(basis_total, AUX_DEV * occupied)
        right_rows = lax.optimization_barrier(right_piece).astype(jnp.float32).transpose(1, 0, 2).reshape(basis_total, AUX_DEV * occupied)
        partial_value = jnp.dot(left_rows, right_rows.T)
        rounded = lax.optimization_barrier(partial_value.astype(jnp.bfloat16)).astype(jnp.float32)
        return summed_exchange + rounded, None

    exchange, _ = lax.scan(add_share, jnp.zeros((basis_total, basis_total), jnp.float32), (left_all, right_all))
    return exchange * (aux_total * occupied) ** -0.5
```

```python
import functools

import jax
import jax.numpy as jnp
from jax import lax
from jax.experimental import pallas as pl
from jax.experimental.pallas import tpu as pltpu
from jax.sharding import PartitionSpec as P

CAP = 2
MESH = pl.DeviceIdType.MESH


def exchange_kernel(
    atoms, auxes, h_ref, fit_ref, out_ref,
    hall, hx, g, epart, cbuf, ybuf,
    local_sem, sx, sz0, sz, rh, sa, ra, sc, rc, sy, ry,
):
    planes, ys = atoms // 2, auxes // 2
    aux_here, rows, occ = h_ref.shape
    me = lax.axis_index("atom")
    ax = lax.axis_index("aux")
    hi, lo = me // 2, me % 2
    y, c = ax // 2, ax % 2
    partner = {"atom": hi * 2 + 1 - lo, "aux": ax}
    peer = {"atom": me, "aux": y * 2 + 1 - c}

    barrier = pltpu.get_barrier_semaphore()

    def greet(device):
        pl.semaphore_signal(barrier, inc=1, device_id=device, device_id_type=MESH)

    greet(partner)
    greet(peer)
    for d in range(1, ys):
        greet({"atom": me, "aux": ((y + d) % ys) * 2 + c})

    @pl.when(hi > 0)
    def _():
        greet({"atom": me - 2, "aux": ax})

    @pl.when(hi < planes - 1)
    def _():
        greet({"atom": me + 2, "aux": ax})

    before = jnp.minimum(hi, 1)
    behind = jnp.minimum(planes - 1 - hi, 1)
    pl.semaphore_wait(barrier, 1 + ys + before + behind)

    def remote(src, dst, send, recv, device):
        return pltpu.make_async_remote_copy(
            src_ref=src, dst_ref=dst, send_sem=send, recv_sem=recv,
            device_id=device, device_id_type=MESH,
        )

    def to_partner(k, atom, src):
        return remote(src, hall.at[atom], sx.at[k], rh.at[atom], partner)

    def along(atom, src, sem, step):
        return remote(src, hall.at[atom], sem, rh.at[atom], {"atom": me + 2 * step, "aux": ax})

    left_ok, right_ok = hi > 0, hi < planes - 1

    @pl.when(left_ok)
    def _():
        along(me, h_ref, sz0.at[0], -1).start()

    @pl.when(right_ok)
    def _():
        along(me, h_ref, sz0.at[1], 1).start()

    to_partner(0, me, h_ref).start()
    for d in range(1, ys):
        remote(h_ref, hx.at[ax], sa.at[d], ra.at[ax], {"atom": me, "aux": ((y + d) % ys) * 2 + c}).start()
    remote(h_ref, hx.at[ax], sa.at[0], ra.at[ax], peer).start()
    own = pltpu.make_async_copy(h_ref, hall.at[me], local_sem.at[0])
    own.start()
    own_aux = pltpu.make_async_copy(h_ref, hx.at[ax], local_sem.at[1])
    own_aux.start()

    def plane_of(k):
        half = (k + 1) // 2
        return hi + half * (1 - 2 * (k % 2))

    def valid(k):
        p = plane_of(k)
        return (p >= 0) & (p < planes) & (k < 2 * planes - 1)

    def forward_ok(k):
        target = hi - (1 - 2 * (k % 2))
        return valid(k) & (target >= 0) & (target < planes)

    def wait_block(atom):
        remote(h_ref, hall.at[atom], sx.at[0], rh.at[atom], partner).wait_recv()

    def relay(k):
        @pl.when(valid(k))
        def _():
            atom = plane_of(k) * 2 + lo
            wait_block(atom)

            @pl.when(forward_ok(k))
            def _():
                along(atom, hall.at[atom], sz.at[k], -(1 - 2 * (k % 2))).start()

            to_partner(k, atom, hall.at[atom]).start()

    relay(1)
    relay(2)

    for d in range(1, ys):
        src = ((y + d) % ys) * 2 + c
        remote(h_ref, hx.at[src], sa.at[0], ra.at[src], peer).wait_recv()
        remote(hx.at[src], hx.at[src], sa.at[ys - 1 + d], ra.at[src], peer).start()
    for d in range(ys):
        src = ((y + d) % ys) * 2 + 1 - c
        remote(h_ref, hx.at[src], sa.at[0], ra.at[src], peer).wait_recv()
    own_aux.wait()
    own.wait()

    piece = 32

    @pl.loop(0, rows // piece)
    def _(j):
        at = pl.ds(pl.multiple_of(j * piece, piece), piece)
        sums = [jnp.zeros((piece, occ), jnp.float32) for _ in range(aux_here)]
        for p in range(aux_here * auxes):
            block = hx[p // aux_here, p % aux_here, at, :].astype(jnp.float32)
            for q in range(aux_here):
                sums[q] = sums[q] + fit_ref[q, p] * block
        for q in range(aux_here):
            g[at, q * occ:(q + 1) * occ] = sums[q].astype(jnp.bfloat16)

    width = 256

    def product(k):
        p = plane_of(k)

        @pl.when(k > 0)
        def _():
            wait_block(p * 2 + 1 - lo)

        @pl.when(k == 0)
        def _():
            wait_block(hi * 2 + 1 - lo)

        for half in range(2):
            @pl.loop(0, rows // width)
            def _(j):
                at = pl.ds(pl.multiple_of(j * width, width), width)
                right = jnp.concatenate(
                    [hall[p * 2 + half, q, at, :] for q in range(aux_here)], axis=-1
                )
                part = lax.dot_general(
                    g[...], right, (((1,), (1,)), ((), ())), preferred_element_type=jnp.float32
                )
                col = pl.ds(pl.multiple_of(half * rows + j * width, width), width)
                epart[p, :, col] = part.astype(jnp.bfloat16)

        @pl.when(p % 2 != c)
        def _():
            remote(epart.at[p], cbuf.at[p // 2], sc.at[p // 2], rc.at[p // 2], peer).start()

    def join(k):
        p = plane_of(k)
        yt = p // 2

        @pl.when(p % 2 == c)
        def _():
            remote(epart.at[p], cbuf.at[yt], sc.at[yt], rc.at[yt], peer).wait_recv()

            @pl.when(yt != y)
            def _():
                @pl.loop(0, rows // 64)
                def _(j):
                    at = pl.ds(pl.multiple_of(j * 64, 64), 64)
                    total = epart[p, at, :].astype(jnp.float32) + cbuf[yt, at, :].astype(jnp.float32)
                    epart[p, at, :] = total.astype(jnp.bfloat16)

                remote(epart.at[p], ybuf.at[y], sy.at[yt], ry.at[y], {"atom": me, "aux": p}).start()

    @pl.loop(0, 2 * planes)
    def _(k):
        @pl.when(valid(k))
        def _():
            product(k)

        @pl.when(k > 0)
        def _():
            @pl.when(valid(k - 1))
            def _():
                join(k - 1)

        relay(k + 3)

    for d in range(1, ys):
        src = (y + d) % ys
        remote(epart.at[ax], ybuf.at[src], sy.at[src], ry.at[src], peer).wait_recv()

    @pl.loop(0, rows // 64)
    def _(j):
        at = pl.ds(pl.multiple_of(j * 64, 64), 64)
        total = epart[ax, at, :].astype(jnp.float32) + cbuf[y, at, :].astype(jnp.float32)
        for d in range(1, ys):
            total = total + ybuf[(y + d) % ys, at, :].astype(jnp.float32)
        out_ref[at, :] = total

    @pl.when(left_ok)
    def _():
        along(me, h_ref, sz0.at[0], -1).wait_send()

    @pl.when(right_ok)
    def _():
        along(me, h_ref, sz0.at[1], 1).wait_send()

    for k in range(2 * planes - 1):
        @pl.when(valid(k))
        def _():
            to_partner(k, me, h_ref).wait_send()

            if k > 0:
                @pl.when(forward_ok(k))
                def _():
                    along(me, h_ref, sz.at[k], -(1 - 2 * (k % 2))).wait_send()

    for d in range(2 * ys - 1):
        remote(h_ref, hx.at[ax], sa.at[d], ra.at[ax], peer).wait_send()
    for t in range(ys):
        remote(epart.at[ax], cbuf.at[t], sc.at[t], rc.at[t], peer).wait_send()
    for d in range(1, ys):
        remote(epart.at[ax], ybuf.at[y], sy.at[(y + d) % ys], ry.at[y], peer).wait_send()


def exchange_call(h, fit_rows):
    aux_here, rows, occ = h.shape
    atoms, auxes = lax.axis_size("atom"), lax.axis_size("aux")
    planes, ys = atoms // 2, auxes // 2
    columns = rows * atoms // auxes
    dma = pltpu.SemaphoreType.DMA
    return pl.pallas_call(
        functools.partial(exchange_kernel, atoms, auxes),
        out_shape=jax.ShapeDtypeStruct((rows, columns), jnp.float32),
        in_specs=[
            pl.BlockSpec(memory_space=pltpu.VMEM),
            pl.BlockSpec(memory_space=pltpu.SMEM),
        ],
        out_specs=pl.BlockSpec(memory_space=pltpu.VMEM),
        scratch_shapes=[
            pltpu.VMEM((atoms, aux_here, rows, occ), jnp.bfloat16),
            pltpu.VMEM((auxes, aux_here, rows, occ), jnp.bfloat16),
            pltpu.VMEM((rows, aux_here * occ), jnp.bfloat16),
            pltpu.VMEM((auxes, rows, columns), jnp.bfloat16),
            pltpu.VMEM((ys, rows, columns), jnp.bfloat16),
            pltpu.VMEM((ys, rows, columns), jnp.bfloat16),
            dma((2,)),
            dma((2 * planes - 1,)),
            dma((2,)),
            dma((2 * planes - 1,)),
            dma((atoms,)),
            dma((2 * ys - 1,)),
            dma((auxes,)),
            dma((ys,)),
            dma((ys,)),
            dma((ys,)),
            dma((ys,)),
        ],
        compiler_params=pltpu.CompilerParams(
            collective_id=0, has_side_effects=True, vmem_limit_bytes=60 * 1024 * 1024
        ),
    )(h, fit_rows)


def per_device(
    three_index, pair_mask, pair_owner, pair_sub, pair_nu, live_count, coefficients, fit_matrix
):
    slot_count, aux_here, block_size, _ = three_index.shape
    rows_here, occupied = coefficients.shape
    blocks_here = rows_here // block_size
    atom_count = lax.axis_size("atom")
    aux_total = fit_matrix.shape[1]
    basis_total = rows_here * atom_count
    shell_size = block_size // pair_mask.shape[1]
    whole_orbitals = lax.all_gather(coefficients, "atom", axis=0, tiled=True)
    orbital_blocks = whole_orbitals.reshape(basis_total // block_size, block_size, occupied)[
        pair_nu
    ]
    expanded = jnp.repeat(jnp.repeat(pair_mask, shell_size, 1), shell_size, 2).astype(jnp.bfloat16)
    masked = three_index * expanded[:, None, :, :]
    halfway = jnp.einsum(
        "tpmn,tni->tpmi", masked, orbital_blocks, preferred_element_type=jnp.float32
    )
    alive_mask = jnp.arange(slot_count) < live_count[0]
    halfway = jnp.where(alive_mask[:, None, None, None], halfway, 0.0).astype(jnp.bfloat16)
    owners = pair_owner[:, 0]
    owner_hits = (owners[:, None] == jnp.arange(atom_count)[None, :]).astype(jnp.int32)
    rank_within = jnp.sum(jnp.cumsum(owner_hits, 0) * owner_hits, 1) - 1
    placement = owners * CAP + rank_within
    routing = (jnp.arange(atom_count * CAP)[:, None] == placement[None, :]).astype(jnp.bfloat16)
    outgoing = jnp.dot(routing, halfway.reshape(slot_count, -1), preferred_element_type=jnp.float32)
    outgoing = outgoing.astype(jnp.bfloat16).reshape(
        atom_count, CAP, aux_here, block_size, occupied
    )
    sub_codes = jnp.dot(
        routing, (pair_sub + 1).astype(jnp.bfloat16)[:, None], preferred_element_type=jnp.float32
    )
    sub_codes = sub_codes.astype(jnp.bfloat16).reshape(atom_count, CAP)
    arrived, arrived_codes = (
        lax.all_to_all(outgoing, "atom", split_axis=0, concat_axis=0, tiled=True),
        lax.all_to_all(sub_codes, "atom", split_axis=0, concat_axis=0, tiled=True),
    )
    wanted = (jnp.arange(blocks_here) + 1).astype(jnp.float32)
    selector = (arrived_codes.reshape(1, -1).astype(jnp.float32) == wanted[:, None]).astype(
        jnp.bfloat16
    )
    gathered_rows = jnp.einsum(
        "sc,cpmi->psmi",
        selector,
        arrived.reshape(atom_count * CAP, aux_here, block_size, occupied),
        preferred_element_type=jnp.float32,
    )
    local_rows = gathered_rows.reshape(aux_here, rows_here, occupied).astype(jnp.bfloat16)
    total = exchange_call(local_rows, fit_matrix.astype(jnp.float32))
    return total * (aux_total * occupied) ** (-0.5)


def solution(mesh):
    in_specs = (
        P("atom", "aux", None, None),
        P("atom", None, None),
        P("atom", None),
        P("atom"),
        P("atom"),
        P("atom"),
        P("atom", None),
        P("aux", None),
    )
    out_specs = P("atom", "aux")
    return jax.shard_map(
        per_device, mesh=mesh, in_specs=in_specs, out_specs=out_specs, check_vma=False
    )
```

```python
import functools

import jax
import jax.numpy as jnp
from jax import lax
from jax.experimental import pallas as pl
from jax.experimental.pallas import tpu as pltpu
from jax.sharding import PartitionSpec as P

CAP = 2
MESH = pl.DeviceIdType.MESH


def exchange_kernel(
    atoms, auxes, h_ref, fit_ref, out_ref,
    hall, hx, g, epart, cbuf, ybuf,
    local_sem, sx, sz0, sz, rh, sa, ra, sc, rc, sy, ry,
):
    planes, ys = atoms // 2, auxes // 2
    aux_here, rows, occ = h_ref.shape
    me = lax.axis_index("atom")
    ax = lax.axis_index("aux")
    hi, lo = me // 2, me % 2
    y, c = ax // 2, ax % 2
    partner = {"atom": hi * 2 + 1 - lo, "aux": ax}
    peer = {"atom": me, "aux": y * 2 + 1 - c}

    barrier = pltpu.get_barrier_semaphore()

    def greet(device):
        pl.semaphore_signal(barrier, inc=1, device_id=device, device_id_type=MESH)

    greet(partner)
    greet(peer)
    for d in range(1, ys):
        greet({"atom": me, "aux": ((y + d) % ys) * 2 + c})

    @pl.when(hi > 0)
    def _():
        greet({"atom": me - 2, "aux": ax})

    @pl.when(hi < planes - 1)
    def _():
        greet({"atom": me + 2, "aux": ax})

    before = jnp.minimum(hi, 1)
    behind = jnp.minimum(planes - 1 - hi, 1)
    pl.semaphore_wait(barrier, 1 + ys + before + behind)

    def remote(src, dst, send, recv, device):
        return pltpu.make_async_remote_copy(
            src_ref=src, dst_ref=dst, send_sem=send, recv_sem=recv,
            device_id=device, device_id_type=MESH,
        )

    def to_partner(k, atom, src):
        return remote(src, hall.at[atom], sx.at[k], rh.at[atom], partner)

    def along(atom, src, sem, step):
        return remote(src, hall.at[atom], sem, rh.at[atom], {"atom": me + 2 * step, "aux": ax})

    left_ok, right_ok = hi > 0, hi < planes - 1

    @pl.when(left_ok)
    def _():
        along(me, h_ref, sz0.at[0], -1).start()

    @pl.when(right_ok)
    def _():
        along(me, h_ref, sz0.at[1], 1).start()

    to_partner(0, me, h_ref).start()
    for d in range(1, ys):
        remote(h_ref, hx.at[ax], sa.at[d], ra.at[ax], {"atom": me, "aux": ((y + d) % ys) * 2 + c}).start()
    remote(h_ref, hx.at[ax], sa.at[0], ra.at[ax], peer).start()
    own = pltpu.make_async_copy(h_ref, hall.at[me], local_sem.at[0])
    own.start()
    own_aux = pltpu.make_async_copy(h_ref, hx.at[ax], local_sem.at[1])
    own_aux.start()

    def plane_of(k):
        half = (k + 1) // 2
        return hi + half * (1 - 2 * (k % 2))

    def valid(k):
        p = plane_of(k)
        return (p >= 0) & (p < planes) & (k < 2 * planes - 1)

    def forward_ok(k):
        target = hi - (1 - 2 * (k % 2))
        return valid(k) & (target >= 0) & (target < planes)

    def wait_block(atom):
        remote(h_ref, hall.at[atom], sx.at[0], rh.at[atom], partner).wait_recv()

    def relay(k):
        @pl.when(valid(k))
        def _():
            atom = plane_of(k) * 2 + lo
            wait_block(atom)

            @pl.when(forward_ok(k))
            def _():
                along(atom, hall.at[atom], sz.at[k], -(1 - 2 * (k % 2))).start()

            to_partner(k, atom, hall.at[atom]).start()

    relay(1)
    relay(2)

    for d in range(1, ys):
        src = ((y + d) % ys) * 2 + c
        remote(h_ref, hx.at[src], sa.at[0], ra.at[src], peer).wait_recv()
        remote(hx.at[src], hx.at[src], sa.at[ys - 1 + d], ra.at[src], peer).start()
    for d in range(ys):
        src = ((y + d) % ys) * 2 + 1 - c
        remote(h_ref, hx.at[src], sa.at[0], ra.at[src], peer).wait_recv()
    own_aux.wait()
    own.wait()

    piece = 32

    @pl.loop(0, rows // piece)
    def _(j):
        at = pl.ds(pl.multiple_of(j * piece, piece), piece)
        sums = [jnp.zeros((piece, occ), jnp.float32) for _ in range(aux_here)]
        for p in range(aux_here * auxes):
            block = hx[p // aux_here, p % aux_here, at, :].astype(jnp.float32)
            for q in range(aux_here):
                sums[q] = sums[q] + fit_ref[q, p] * block
        for q in range(aux_here):
            g[at, q * occ:(q + 1) * occ] = sums[q].astype(jnp.bfloat16)

    width = 256

    def product(k):
        p = plane_of(k)

        @pl.when(k > 0)
        def _():
            wait_block(p * 2 + 1 - lo)

        @pl.when(k == 0)
        def _():
            wait_block(hi * 2 + 1 - lo)

        for half in range(2):
            @pl.loop(0, rows // width)
            def _(j):
                at = pl.ds(pl.multiple_of(j * width, width), width)
                right = jnp.concatenate(
                    [hall[p * 2 + half, q, at, :] for q in range(aux_here)], axis=-1
                )
                part = lax.dot_general(
                    g[...], right, (((1,), (1,)), ((), ())), preferred_element_type=jnp.float32
                )
                col = pl.ds(pl.multiple_of(half * rows + j * width, width), width)
                epart[p, :, col] = part.astype(jnp.bfloat16)

        @pl.when(p % 2 != c)
        def _():
            remote(epart.at[p], cbuf.at[p // 2], sc.at[p // 2], rc.at[p // 2], peer).start()

    def join(k):
        p = plane_of(k)
        yt = p // 2

        @pl.when(p % 2 == c)
        def _():
            remote(epart.at[p], cbuf.at[yt], sc.at[yt], rc.at[yt], peer).wait_recv()

            @pl.when(yt != y)
            def _():
                @pl.loop(0, rows // 64)
                def _(j):
                    at = pl.ds(pl.multiple_of(j * 64, 64), 64)
                    total = epart[p, at, :].astype(jnp.float32) + cbuf[yt, at, :].astype(jnp.float32)
                    epart[p, at, :] = total.astype(jnp.bfloat16)

                remote(epart.at[p], ybuf.at[y], sy.at[yt], ry.at[y], {"atom": me, "aux": p}).start()

    @pl.loop(0, 2 * planes)
    def _(k):
        @pl.when(valid(k))
        def _():
            product(k)

        @pl.when(k > 0)
        def _():
            @pl.when(valid(k - 1))
            def _():
                join(k - 1)

        relay(k + 3)

    for d in range(1, ys):
        src = (y + d) % ys
        remote(epart.at[ax], ybuf.at[src], sy.at[src], ry.at[src], peer).wait_recv()

    @pl.loop(0, rows // 64)
    def _(j):
        at = pl.ds(pl.multiple_of(j * 64, 64), 64)
        total = epart[ax, at, :].astype(jnp.float32) + cbuf[y, at, :].astype(jnp.float32)
        for d in range(1, ys):
            total = total + ybuf[(y + d) % ys, at, :].astype(jnp.float32)
        out_ref[at, :] = total

    @pl.when(left_ok)
    def _():
        along(me, h_ref, sz0.at[0], -1).wait_send()

    @pl.when(right_ok)
    def _():
        along(me, h_ref, sz0.at[1], 1).wait_send()

    for k in range(2 * planes - 1):
        @pl.when(valid(k))
        def _():
            to_partner(k, me, h_ref).wait_send()

            if k > 0:
                @pl.when(forward_ok(k))
                def _():
                    along(me, h_ref, sz.at[k], -(1 - 2 * (k % 2))).wait_send()

    for d in range(2 * ys - 1):
        remote(h_ref, hx.at[ax], sa.at[d], ra.at[ax], peer).wait_send()
    for t in range(ys):
        remote(epart.at[ax], cbuf.at[t], sc.at[t], rc.at[t], peer).wait_send()
    for d in range(1, ys):
        remote(epart.at[ax], ybuf.at[y], sy.at[(y + d) % ys], ry.at[y], peer).wait_send()


def exchange_call(h, fit_rows):
    aux_here, rows, occ = h.shape
    atoms, auxes = lax.axis_size("atom"), lax.axis_size("aux")
    planes, ys = atoms // 2, auxes // 2
    columns = rows * atoms // auxes
    dma = pltpu.SemaphoreType.DMA
    return pl.pallas_call(
        functools.partial(exchange_kernel, atoms, auxes),
        out_shape=jax.ShapeDtypeStruct((rows, columns), jnp.float32),
        in_specs=[
            pl.BlockSpec(memory_space=pltpu.VMEM),
            pl.BlockSpec(memory_space=pltpu.SMEM),
        ],
        out_specs=pl.BlockSpec(memory_space=pltpu.VMEM),
        scratch_shapes=[
            pltpu.VMEM((atoms, aux_here, rows, occ), jnp.bfloat16),
            pltpu.VMEM((auxes, aux_here, rows, occ), jnp.bfloat16),
            pltpu.VMEM((rows, aux_here * occ), jnp.bfloat16),
            pltpu.VMEM((auxes, rows, columns), jnp.bfloat16),
            pltpu.VMEM((ys, rows, columns), jnp.bfloat16),
            pltpu.VMEM((ys, rows, columns), jnp.bfloat16),
            dma((2,)),
            dma((2 * planes - 1,)),
            dma((2,)),
            dma((2 * planes - 1,)),
            dma((atoms,)),
            dma((2 * ys - 1,)),
            dma((auxes,)),
            dma((ys,)),
            dma((ys,)),
            dma((ys,)),
            dma((ys,)),
        ],
        compiler_params=pltpu.CompilerParams(
            collective_id=0, has_side_effects=True, vmem_limit_bytes=60 * 1024 * 1024
        ),
    )(h, fit_rows)


def route_kernel(
    atoms, order_ref, nu_ref, three_ref, mask_ref, code_ref, own_ref, out_ref,
    orbitals, outgoing, arrived, codes, acc,
    local_sem, sx, sz0, sz, rh, sd, rd, sk, rk,
):
    planes, middle = atoms // 2, atoms // 2
    cap = code_ref.shape[1]
    per, size, occ = own_ref.shape
    aux_here = three_ref.shape[1]
    me = lax.axis_index("atom")
    ax = lax.axis_index("aux")
    hi, lo = me // 2, me % 2
    side, pos = me // middle, me % middle

    def at_atom(atom):
        return {"atom": atom, "aux": ax}

    barrier = pltpu.get_barrier_semaphore()
    for d in range(1, atoms):
        pl.semaphore_signal(
            barrier, inc=1, device_id=at_atom((me + d) % atoms), device_id_type=MESH
        )
    pl.semaphore_wait(barrier, atoms - 1)

    def remote(src, dst, send, recv, device):
        return pltpu.make_async_remote_copy(
            src_ref=src, dst_ref=dst, send_sem=send, recv_sem=recv,
            device_id=device, device_id_type=MESH,
        )

    def spot(atom):
        return orbitals.at[pl.ds(atom * per, per)]

    def to_partner(k, atom, src):
        return remote(src, spot(atom), sx.at[k], rh.at[atom], at_atom(hi * 2 + 1 - lo))

    def along(atom, src, sem, step):
        return remote(src, spot(atom), sem, rh.at[atom], at_atom(me + 2 * step))

    left_ok, right_ok = hi > 0, hi < planes - 1

    @pl.when(left_ok)
    def _():
        along(me, own_ref, sz0.at[0], -1).start()

    @pl.when(right_ok)
    def _():
        along(me, own_ref, sz0.at[1], 1).start()

    to_partner(0, me, own_ref).start()
    own = pltpu.make_async_copy(own_ref, spot(me), local_sem.at[0])
    own.start()

    def plane_of(k):
        half = (k + 1) // 2
        return hi + half * (1 - 2 * (k % 2))

    def valid(k):
        p = plane_of(k)
        return (p >= 0) & (p < planes)

    def forward_ok(k):
        target = hi - (1 - 2 * (k % 2))
        return valid(k) & (target >= 0) & (target < planes)

    def wait_block(atom):
        remote(own_ref, spot(atom), sx.at[0], rh.at[atom], at_atom(hi * 2 + 1 - lo)).wait_recv()

    @pl.loop(1, 2 * planes - 1)
    def _(k):
        @pl.when(valid(k))
        def _():
            atom = plane_of(k) * 2 + lo
            wait_block(atom)

            @pl.when(forward_ok(k))
            def _():
                along(atom, spot(atom), sz.at[k], -(1 - 2 * (k % 2))).start()

            to_partner(k, atom, spot(atom)).start()

    @pl.loop(0, planes)
    def _(p):
        wait_block(p * 2 + 1 - lo)

    own.wait()

    def half_block(place):
        slot, nu = order_ref[place], nu_ref[place]
        right = orbitals[nu]
        left = three_ref[slot] * mask_ref[slot][None, :, :]
        value = jnp.dot(
            left.reshape(aux_here * size, size), right, preferred_element_type=jnp.float32
        )
        return value.reshape(aux_here, size, occ).astype(jnp.bfloat16)

    def target_of(j):
        far = (1 - side) * middle + (pos + j) % middle
        near = side * middle + (pos + j + 1) % middle
        return jnp.where(j < middle, far, near)

    @pl.loop(0, atoms - 1)
    def _(j):
        target = target_of(j)

        @pl.loop(0, cap)
        def _(r):
            outgoing[j, r] = half_block(target * cap + r)

        remote(outgoing.at[j], arrived.at[me], sd.at[j], rd.at[me], at_atom(target)).start()
        remote(code_ref.at[target], codes.at[me], sk.at[j], rk.at[me], at_atom(target)).start()

    @pl.loop(0, cap)
    def _(r):
        arrived[me, r] = half_block(me * cap + r)

    keep = pltpu.make_async_copy(code_ref.at[me], codes.at[me], local_sem.at[1])
    keep.start()
    keep.wait()
    acc[...] = jnp.zeros_like(acc)

    def take(src):
        hits = [
            [codes[src, r, b] for r in range(cap)]
            for b in range(per)
        ]

        @pl.loop(0, aux_here * (size // 64))
        def _(n):
            p, part = n // (size // 64), n % (size // 64)
            at = pl.ds(pl.multiple_of(part * 64, 64), 64)
            values = [
                arrived[src, r, p, at, :].astype(jnp.float32).reshape(8, 8, occ)
                for r in range(cap)
            ]
            for b in range(per):
                to = pl.ds(pl.multiple_of(b * size + part * 64, 64), 64)
                total = acc[p, to, :].reshape(8, 8, occ)
                for r in range(cap):
                    total = total + values[r] * hits[b][r][None]
                acc[p, to, :] = total.reshape(64, occ)

    take(me)

    @pl.loop(0, atoms - 1)
    def _(j):
        near = side * middle + (pos + j + 1) % middle
        far = (1 - side) * middle + (pos + 2 * middle - 1 - j) % middle
        src = jnp.where(j < middle - 1, near, far)
        remote(outgoing.at[0], arrived.at[src], sd.at[0], rd.at[src], at_atom(src)).wait_recv()
        remote(code_ref.at[0], codes.at[src], sk.at[0], rk.at[src], at_atom(src)).wait_recv()
        take(src)

    out_ref[...] = acc[...].astype(jnp.bfloat16)

    @pl.when(left_ok)
    def _():
        along(me, own_ref, sz0.at[0], -1).wait_send()

    @pl.when(right_ok)
    def _():
        along(me, own_ref, sz0.at[1], 1).wait_send()

    to_partner(0, me, own_ref).wait_send()

    @pl.loop(1, 2 * planes - 1)
    def _(k):
        @pl.when(valid(k))
        def _():
            to_partner(k, me, own_ref).wait_send()

            @pl.when(forward_ok(k))
            def _():
                along(me, own_ref, sz.at[k], -(1 - 2 * (k % 2))).wait_send()

    @pl.loop(0, atoms - 1)
    def _(j):
        target = target_of(j)
        remote(outgoing.at[j], arrived.at[me], sd.at[j], rd.at[me], at_atom(target)).wait_send()
        remote(code_ref.at[target], codes.at[me], sk.at[j], rk.at[me], at_atom(target)).wait_send()


def route_call(order, nu, three_index, mask, codes, coefficients):
    aux_here, size = three_index.shape[1], three_index.shape[2]
    rows, occ = coefficients.shape
    per = rows // size
    atoms = lax.axis_size("atom")
    planes = atoms // 2
    dma = pltpu.SemaphoreType.DMA
    smem = pl.BlockSpec(memory_space=pltpu.SMEM)
    vmem = pl.BlockSpec(memory_space=pltpu.VMEM)
    return pl.pallas_call(
        functools.partial(route_kernel, atoms),
        out_shape=jax.ShapeDtypeStruct((aux_here, rows, occ), jnp.bfloat16),
        in_specs=[smem, smem, vmem, vmem, vmem, vmem],
        out_specs=vmem,
        scratch_shapes=[
            pltpu.VMEM((atoms * per, size, occ), jnp.bfloat16),
            pltpu.VMEM((atoms - 1, CAP, aux_here, size, occ), jnp.bfloat16),
            pltpu.VMEM((atoms, CAP, aux_here, size, occ), jnp.bfloat16),
            pltpu.VMEM((atoms, CAP, per, 8, 128), jnp.float32),
            pltpu.VMEM((aux_here, rows, occ), jnp.float32),
            dma((2,)),
            dma((2 * planes - 1,)),
            dma((2,)),
            dma((2 * planes - 1,)),
            dma((atoms,)),
            dma((atoms - 1,)),
            dma((atoms,)),
            dma((atoms - 1,)),
            dma((atoms,)),
        ],
        compiler_params=pltpu.CompilerParams(
            collective_id=1, has_side_effects=True, vmem_limit_bytes=60 * 1024 * 1024
        ),
    )(order, nu, three_index, mask, codes, coefficients.reshape(per, size, occ))


def per_device(
    three_index, pair_mask, pair_owner, pair_sub, pair_nu, live_count, coefficients, fit_matrix
):
    slot_count, aux_here, block_size, _ = three_index.shape
    rows_here, occupied = coefficients.shape
    atom_count = lax.axis_size("atom")
    aux_total = fit_matrix.shape[1]
    shell_size = block_size // pair_mask.shape[1]
    expanded = jnp.repeat(jnp.repeat(pair_mask, shell_size, 1), shell_size, 2).astype(jnp.bfloat16)
    owners = pair_owner[:, 0]
    owner_hits = (owners[:, None] == jnp.arange(atom_count)[None, :]).astype(jnp.int32)
    rank_within = jnp.sum(jnp.cumsum(owner_hits, 0) * owner_hits, 1) - 1
    placement = owners * CAP + rank_within
    routing = (jnp.arange(atom_count * CAP)[:, None] == placement[None, :]).astype(jnp.int32)
    slots = jnp.arange(slot_count, dtype=jnp.int32)

    def placed(values):
        return jnp.sum(routing * values[None, :], 1)

    live_codes = placed(jnp.where(slots < live_count[0], pair_sub + 1, 0))
    blocks = jnp.arange(rows_here // block_size)
    hits = (live_codes[:, None] == blocks[None, :] + 1).astype(jnp.float32)
    hits = hits.reshape(atom_count, CAP, blocks.shape[0], 1, 1)
    local_rows = route_call(
        placed(slots),
        placed(pair_nu),
        three_index,
        expanded,
        jnp.broadcast_to(hits, hits.shape[:3] + (8, 128)),
        coefficients,
    )
    total = exchange_call(local_rows, fit_matrix.astype(jnp.float32))
    return total * (aux_total * occupied) ** (-0.5)


def solution(mesh):
    in_specs = (
        P("atom", "aux", None, None),
        P("atom", None, None),
        P("atom", None),
        P("atom"),
        P("atom"),
        P("atom"),
        P("atom", None),
        P("aux", None),
    )
    out_specs = P("atom", "aux")
    return jax.shard_map(
        per_device, mesh=mesh, in_specs=in_specs, out_specs=out_specs, check_vma=False
    )
```

```python
import functools

import jax
import jax.numpy as jnp
from jax import lax
from jax.experimental import pallas as pl
from jax.experimental.pallas import tpu as pltpu
from jax.sharding import PartitionSpec as P

CAP = 2
MESH = pl.DeviceIdType.MESH


def exchange_kernel(
    atoms, auxes, h_ref, fit_ref, out_ref,
    hall, hx, g, epart, cbuf, ybuf,
    local_sem, sx, sz0, sz, rh, sa, ra, sc, rc, sy, ry,
):
    planes, ys = atoms // 2, auxes // 2
    aux_here, rows, occ = h_ref.shape
    me = lax.axis_index("atom")
    ax = lax.axis_index("aux")
    hi, lo = me // 2, me % 2
    y, c = ax // 2, ax % 2
    partner = {"atom": hi * 2 + 1 - lo, "aux": ax}
    peer = {"atom": me, "aux": y * 2 + 1 - c}

    barrier = pltpu.get_barrier_semaphore()

    def greet(device):
        pl.semaphore_signal(barrier, inc=1, device_id=device, device_id_type=MESH)

    greet(partner)
    greet(peer)
    for d in range(1, ys):
        greet({"atom": me, "aux": ((y + d) % ys) * 2 + c})

    @pl.when(hi > 0)
    def _():
        greet({"atom": me - 2, "aux": ax})

    @pl.when(hi < planes - 1)
    def _():
        greet({"atom": me + 2, "aux": ax})

    before = jnp.minimum(hi, 1)
    behind = jnp.minimum(planes - 1 - hi, 1)
    pl.semaphore_wait(barrier, 1 + ys + before + behind)

    def remote(src, dst, send, recv, device):
        return pltpu.make_async_remote_copy(
            src_ref=src, dst_ref=dst, send_sem=send, recv_sem=recv,
            device_id=device, device_id_type=MESH,
        )

    def to_partner(k, atom, src):
        return remote(src, hall.at[atom], sx.at[k], rh.at[atom], partner)

    def along(atom, src, sem, step):
        return remote(src, hall.at[atom], sem, rh.at[atom], {"atom": me + 2 * step, "aux": ax})

    left_ok, right_ok = hi > 0, hi < planes - 1

    @pl.when(left_ok)
    def _():
        along(me, h_ref, sz0.at[0], -1).start()

    @pl.when(right_ok)
    def _():
        along(me, h_ref, sz0.at[1], 1).start()

    to_partner(0, me, h_ref).start()
    for d in range(1, ys):
        remote(h_ref, hx.at[ax], sa.at[d], ra.at[ax], {"atom": me, "aux": ((y + d) % ys) * 2 + c}).start()
    remote(h_ref, hx.at[ax], sa.at[0], ra.at[ax], peer).start()
    own = pltpu.make_async_copy(h_ref, hall.at[me], local_sem.at[0])
    own.start()
    own_aux = pltpu.make_async_copy(h_ref, hx.at[ax], local_sem.at[1])
    own_aux.start()

    def plane_of(k):
        half = (k + 1) // 2
        return hi + half * (1 - 2 * (k % 2))

    def valid(k):
        p = plane_of(k)
        return (p >= 0) & (p < planes) & (k < 2 * planes - 1)

    def forward_ok(k):
        target = hi - (1 - 2 * (k % 2))
        return valid(k) & (target >= 0) & (target < planes)

    def wait_block(atom):
        remote(h_ref, hall.at[atom], sx.at[0], rh.at[atom], partner).wait_recv()

    def relay(k):
        @pl.when(valid(k))
        def _():
            atom = plane_of(k) * 2 + lo
            wait_block(atom)

            @pl.when(forward_ok(k))
            def _():
                along(atom, hall.at[atom], sz.at[k], -(1 - 2 * (k % 2))).start()

            to_partner(k, atom, hall.at[atom]).start()

    relay(1)
    relay(2)

    for d in range(1, ys):
        src = ((y + d) % ys) * 2 + c
        remote(h_ref, hx.at[src], sa.at[0], ra.at[src], peer).wait_recv()
        remote(hx.at[src], hx.at[src], sa.at[ys - 1 + d], ra.at[src], peer).start()
    for d in range(ys):
        src = ((y + d) % ys) * 2 + 1 - c
        remote(h_ref, hx.at[src], sa.at[0], ra.at[src], peer).wait_recv()
    own_aux.wait()
    own.wait()

    piece = 32

    @pl.loop(0, rows // piece)
    def _(j):
        at = pl.ds(pl.multiple_of(j * piece, piece), piece)
        sums = [jnp.zeros((piece, occ), jnp.float32) for _ in range(aux_here)]
        for p in range(aux_here * auxes):
            block = hx[p // aux_here, p % aux_here, at, :].astype(jnp.float32)
            for q in range(aux_here):
                sums[q] = sums[q] + fit_ref[q, p] * block
        for q in range(aux_here):
            g[at, q * occ:(q + 1) * occ] = sums[q].astype(jnp.bfloat16)

    width = 256

    def product(k):
        p = plane_of(k)

        @pl.when(k > 0)
        def _():
            wait_block(p * 2 + 1 - lo)

        @pl.when(k == 0)
        def _():
            wait_block(hi * 2 + 1 - lo)

        for half in range(2):
            @pl.loop(0, rows // width)
            def _(j):
                at = pl.ds(pl.multiple_of(j * width, width), width)
                right = jnp.concatenate(
                    [hall[p * 2 + half, q, at, :] for q in range(aux_here)], axis=-1
                )
                part = lax.dot_general(
                    g[...], right, (((1,), (1,)), ((), ())), preferred_element_type=jnp.float32
                )
                col = pl.ds(pl.multiple_of(half * rows + j * width, width), width)
                epart[p, :, col] = part.astype(jnp.bfloat16)

        @pl.when(p % 2 != c)
        def _():
            remote(epart.at[p], cbuf.at[p // 2], sc.at[p // 2], rc.at[p // 2], peer).start()

    def join(k):
        p = plane_of(k)
        yt = p // 2

        @pl.when(p % 2 == c)
        def _():
            remote(epart.at[p], cbuf.at[yt], sc.at[yt], rc.at[yt], peer).wait_recv()

            @pl.when(yt != y)
            def _():
                @pl.loop(0, rows // 64)
                def _(j):
                    at = pl.ds(pl.multiple_of(j * 64, 64), 64)
                    total = epart[p, at, :].astype(jnp.float32) + cbuf[yt, at, :].astype(jnp.float32)
                    epart[p, at, :] = total.astype(jnp.bfloat16)

                remote(epart.at[p], ybuf.at[y], sy.at[yt], ry.at[y], {"atom": me, "aux": p}).start()

    @pl.loop(0, 2 * planes)
    def _(k):
        @pl.when(valid(k))
        def _():
            product(k)

        @pl.when(k > 0)
        def _():
            @pl.when(valid(k - 1))
            def _():
                join(k - 1)

        relay(k + 3)

    for d in range(1, ys):
        src = (y + d) % ys
        remote(epart.at[ax], ybuf.at[src], sy.at[src], ry.at[src], peer).wait_recv()

    @pl.loop(0, rows // 64)
    def _(j):
        at = pl.ds(pl.multiple_of(j * 64, 64), 64)
        total = epart[ax, at, :].astype(jnp.float32) + cbuf[y, at, :].astype(jnp.float32)
        for d in range(1, ys):
            total = total + ybuf[(y + d) % ys, at, :].astype(jnp.float32)
        out_ref[at, :] = total

    @pl.when(left_ok)
    def _():
        along(me, h_ref, sz0.at[0], -1).wait_send()

    @pl.when(right_ok)
    def _():
        along(me, h_ref, sz0.at[1], 1).wait_send()

    for k in range(2 * planes - 1):
        @pl.when(valid(k))
        def _():
            to_partner(k, me, h_ref).wait_send()

            if k > 0:
                @pl.when(forward_ok(k))
                def _():
                    along(me, h_ref, sz.at[k], -(1 - 2 * (k % 2))).wait_send()

    for d in range(2 * ys - 1):
        remote(h_ref, hx.at[ax], sa.at[d], ra.at[ax], peer).wait_send()
    for t in range(ys):
        remote(epart.at[ax], cbuf.at[t], sc.at[t], rc.at[t], peer).wait_send()
    for d in range(1, ys):
        remote(epart.at[ax], ybuf.at[y], sy.at[(y + d) % ys], ry.at[y], peer).wait_send()


def exchange_call(h, fit_rows):
    aux_here, rows, occ = h.shape
    atoms, auxes = lax.axis_size("atom"), lax.axis_size("aux")
    planes, ys = atoms // 2, auxes // 2
    columns = rows * atoms // auxes
    dma = pltpu.SemaphoreType.DMA
    return pl.pallas_call(
        functools.partial(exchange_kernel, atoms, auxes),
        out_shape=jax.ShapeDtypeStruct((rows, columns), jnp.float32),
        in_specs=[
            pl.BlockSpec(memory_space=pltpu.VMEM),
            pl.BlockSpec(memory_space=pltpu.SMEM),
        ],
        out_specs=pl.BlockSpec(memory_space=pltpu.VMEM),
        scratch_shapes=[
            pltpu.VMEM((atoms, aux_here, rows, occ), jnp.bfloat16),
            pltpu.VMEM((auxes, aux_here, rows, occ), jnp.bfloat16),
            pltpu.VMEM((rows, aux_here * occ), jnp.bfloat16),
            pltpu.VMEM((auxes, rows, columns), jnp.bfloat16),
            pltpu.VMEM((ys, rows, columns), jnp.bfloat16),
            pltpu.VMEM((ys, rows, columns), jnp.bfloat16),
            dma((2,)),
            dma((2 * planes - 1,)),
            dma((2,)),
            dma((2 * planes - 1,)),
            dma((atoms,)),
            dma((2 * ys - 1,)),
            dma((auxes,)),
            dma((ys,)),
            dma((ys,)),
            dma((ys,)),
            dma((ys,)),
        ],
        compiler_params=pltpu.CompilerParams(
            collective_id=0, has_side_effects=True, vmem_limit_bytes=60 * 1024 * 1024
        ),
    )(h, fit_rows)


def route_kernel(
    atoms, order_ref, nu_ref, three_ref, mask_ref, code_ref, own_ref, out_ref,
    orbitals, outgoing, arrived, codes, acc, summed, landed,
    local_sem, sx, sz0, sz, rh, sd, rd, sk, rk, cross_sem,
):
    planes, middle = atoms // 2, atoms // 2
    cap = code_ref.shape[1]
    per, size, occ = own_ref.shape
    aux_here = three_ref.shape[1]
    me = lax.axis_index("atom")
    ax = lax.axis_index("aux")
    hi, lo = me // 2, me % 2
    side, pos = me // middle, me % middle

    def at_atom(atom):
        return {"atom": atom, "aux": ax}

    barrier = pltpu.get_barrier_semaphore()
    for d in range(1, atoms):
        pl.semaphore_signal(
            barrier, inc=1, device_id=at_atom((me + d) % atoms), device_id_type=MESH
        )
    pl.semaphore_wait(barrier, atoms - 1)

    def remote(src, dst, send, recv, device):
        return pltpu.make_async_remote_copy(
            src_ref=src, dst_ref=dst, send_sem=send, recv_sem=recv,
            device_id=device, device_id_type=MESH,
        )

    def spot(atom):
        return orbitals.at[pl.ds(atom * per, per)]

    def to_partner(k, atom, src):
        return remote(src, spot(atom), sx.at[k], rh.at[atom], at_atom(hi * 2 + 1 - lo))

    def along(atom, src, sem, step):
        return remote(src, spot(atom), sem, rh.at[atom], at_atom(me + 2 * step))

    left_ok, right_ok = hi > 0, hi < planes - 1

    @pl.when(left_ok)
    def _():
        along(me, own_ref, sz0.at[0], -1).start()

    @pl.when(right_ok)
    def _():
        along(me, own_ref, sz0.at[1], 1).start()

    to_partner(0, me, own_ref).start()
    own = pltpu.make_async_copy(own_ref, spot(me), local_sem.at[0])
    own.start()

    def plane_of(k):
        half = (k + 1) // 2
        return hi + half * (1 - 2 * (k % 2))

    def valid(k):
        p = plane_of(k)
        return (p >= 0) & (p < planes)

    def forward_ok(k):
        target = hi - (1 - 2 * (k % 2))
        return valid(k) & (target >= 0) & (target < planes)

    def wait_block(atom):
        remote(own_ref, spot(atom), sx.at[0], rh.at[atom], at_atom(hi * 2 + 1 - lo)).wait_recv()

    @pl.loop(1, 2 * planes - 1)
    def _(k):
        @pl.when(valid(k))
        def _():
            atom = plane_of(k) * 2 + lo
            wait_block(atom)

            @pl.when(forward_ok(k))
            def _():
                along(atom, spot(atom), sz.at[k], -(1 - 2 * (k % 2))).start()

            to_partner(k, atom, spot(atom)).start()

    @pl.loop(0, planes)
    def _(p):
        wait_block(p * 2 + 1 - lo)

    own.wait()

    def half_block(place):
        slot, nu = order_ref[place], nu_ref[place]
        right = orbitals[nu]
        left = three_ref[slot] * mask_ref[slot][None, :, :]
        value = jnp.dot(
            left.reshape(aux_here * size, size), right, preferred_element_type=jnp.float32
        )
        return value.reshape(aux_here, size, occ).astype(jnp.bfloat16)

    def target_of(j):
        return (pos + j % (middle - 1) + 1) % middle

    def start_sends(first, owner_side):
        @pl.loop(first, first + middle - 1)
        def _(j):
            q = target_of(j)
            owner = owner_side * middle + q
            lane = (first // (middle - 1)) * middle + pos

            @pl.loop(0, cap)
            def _(r):
                outgoing[j, r] = half_block(owner * cap + r)

            device = at_atom(side * middle + q)
            remote(outgoing.at[j], arrived.at[lane], sd.at[j], rd.at[lane], device).start()
            remote(code_ref.at[owner], codes.at[lane], sk.at[j], rk.at[lane], device).start()

    def fill_own(lane, owner, sem):
        @pl.loop(0, cap)
        def _(r):
            arrived[lane, r] = half_block(owner * cap + r)

        keep = pltpu.make_async_copy(code_ref.at[owner], codes.at[lane], sem)
        keep.start()
        keep.wait()

    start_sends(0, 1 - side)
    fill_own(pos, (1 - side) * middle + pos, local_sem.at[1])
    start_sends(middle - 1, side)
    fill_own(middle + pos, me, local_sem.at[2])

    def take(src):
        hits = [
            [codes[src, r, b] for r in range(cap)]
            for b in range(per)
        ]

        @pl.loop(0, aux_here * (size // 64))
        def _(n):
            p, part = n // (size // 64), n % (size // 64)
            at = pl.ds(pl.multiple_of(part * 64, 64), 64)
            values = [
                arrived[src, r, p, at, :].astype(jnp.float32).reshape(8, 8, occ)
                for r in range(cap)
            ]
            for b in range(per):
                to = pl.ds(pl.multiple_of(b * size + part * 64, 64), 64)
                total = acc[p, to, :].reshape(8, 8, occ)
                for r in range(cap):
                    total = total + values[r] * hits[b][r][None]
                acc[p, to, :] = total.reshape(64, occ)

    def take_all(base):
        acc[...] = jnp.zeros_like(acc)
        take(base + pos)

        @pl.loop(1, middle)
        def _(i):
            src = (pos + middle - i) % middle
            lane = base + src
            device = at_atom(side * middle + src)
            remote(outgoing.at[0], arrived.at[lane], sd.at[0], rd.at[lane], device).wait_recv()
            remote(code_ref.at[0], codes.at[lane], sk.at[0], rk.at[lane], device).wait_recv()
            take(lane)

    across = at_atom((1 - side) * middle + pos)
    take_all(0)
    summed[...] = acc[...].astype(jnp.bfloat16)
    cross = remote(summed, landed, cross_sem.at[0], cross_sem.at[1], across)
    cross.start()
    take_all(middle)
    cross.wait_recv()
    out_ref[...] = (acc[...] + landed[...].astype(jnp.float32)).astype(jnp.bfloat16)
    cross.wait_send()

    @pl.when(left_ok)
    def _():
        along(me, own_ref, sz0.at[0], -1).wait_send()

    @pl.when(right_ok)
    def _():
        along(me, own_ref, sz0.at[1], 1).wait_send()

    to_partner(0, me, own_ref).wait_send()

    @pl.loop(1, 2 * planes - 1)
    def _(k):
        @pl.when(valid(k))
        def _():
            to_partner(k, me, own_ref).wait_send()

            @pl.when(forward_ok(k))
            def _():
                along(me, own_ref, sz.at[k], -(1 - 2 * (k % 2))).wait_send()

    @pl.loop(0, 2 * middle - 2)
    def _(j):
        device = at_atom(side * middle + target_of(j))
        remote(outgoing.at[j], arrived.at[0], sd.at[j], rd.at[0], device).wait_send()
        remote(code_ref.at[0], codes.at[0], sk.at[j], rk.at[0], device).wait_send()


def route_call(order, nu, three_index, mask, codes, coefficients):
    aux_here, size = three_index.shape[1], three_index.shape[2]
    rows, occ = coefficients.shape
    per = rows // size
    atoms = lax.axis_size("atom")
    planes = atoms // 2
    dma = pltpu.SemaphoreType.DMA
    smem = pl.BlockSpec(memory_space=pltpu.SMEM)
    vmem = pl.BlockSpec(memory_space=pltpu.VMEM)
    return pl.pallas_call(
        functools.partial(route_kernel, atoms),
        out_shape=jax.ShapeDtypeStruct((aux_here, rows, occ), jnp.bfloat16),
        in_specs=[smem, smem, vmem, vmem, vmem, vmem],
        out_specs=vmem,
        scratch_shapes=[
            pltpu.VMEM((atoms * per, size, occ), jnp.bfloat16),
            pltpu.VMEM((atoms - 2, CAP, aux_here, size, occ), jnp.bfloat16),
            pltpu.VMEM((atoms, CAP, aux_here, size, occ), jnp.bfloat16),
            pltpu.VMEM((atoms, CAP, per, 8, 128), jnp.float32),
            pltpu.VMEM((aux_here, rows, occ), jnp.float32),
            pltpu.VMEM((aux_here, rows, occ), jnp.bfloat16),
            pltpu.VMEM((aux_here, rows, occ), jnp.bfloat16),
            dma((3,)),
            dma((2 * planes - 1,)),
            dma((2,)),
            dma((2 * planes - 1,)),
            dma((atoms,)),
            dma((atoms - 2,)),
            dma((atoms,)),
            dma((atoms - 2,)),
            dma((atoms,)),
            dma((2,)),
        ],
        compiler_params=pltpu.CompilerParams(
            collective_id=1, has_side_effects=True, vmem_limit_bytes=60 * 1024 * 1024
        ),
    )(order, nu, three_index, mask, codes, coefficients.reshape(per, size, occ))


def per_device(
    three_index, pair_mask, pair_owner, pair_sub, pair_nu, live_count, coefficients, fit_matrix
):
    slot_count, aux_here, block_size, _ = three_index.shape
    rows_here, occupied = coefficients.shape
    atom_count = lax.axis_size("atom")
    aux_total = fit_matrix.shape[1]
    shell_size = block_size // pair_mask.shape[1]
    expanded = jnp.repeat(jnp.repeat(pair_mask, shell_size, 1), shell_size, 2).astype(jnp.bfloat16)
    owners = pair_owner[:, 0]
    owner_hits = (owners[:, None] == jnp.arange(atom_count)[None, :]).astype(jnp.int32)
    rank_within = jnp.sum(jnp.cumsum(owner_hits, 0) * owner_hits, 1) - 1
    placement = owners * CAP + rank_within
    routing = (jnp.arange(atom_count * CAP)[:, None] == placement[None, :]).astype(jnp.int32)
    slots = jnp.arange(slot_count, dtype=jnp.int32)

    def placed(values):
        return jnp.sum(routing * values[None, :], 1)

    live_codes = placed(jnp.where(slots < live_count[0], pair_sub + 1, 0))
    blocks = jnp.arange(rows_here // block_size)
    hits = (live_codes[:, None] == blocks[None, :] + 1).astype(jnp.float32)
    hits = hits.reshape(atom_count, CAP, blocks.shape[0], 1, 1)
    local_rows = route_call(
        placed(slots),
        placed(pair_nu),
        three_index,
        expanded,
        jnp.broadcast_to(hits, hits.shape[:3] + (8, 128)),
        coefficients,
    )
    total = exchange_call(local_rows, fit_matrix.astype(jnp.float32))
    return total * (aux_total * occupied) ** (-0.5)


def solution(mesh):
    in_specs = (
        P("atom", "aux", None, None),
        P("atom", None, None),
        P("atom", None),
        P("atom"),
        P("atom"),
        P("atom"),
        P("atom", None),
        P("aux", None),
    )
    out_specs = P("atom", "aux")
    return jax.shard_map(
        per_device, mesh=mesh, in_specs=in_specs, out_specs=out_specs, check_vma=False
    )
```

```python
import functools

import jax
import jax.numpy as jnp
from jax import lax
from jax.experimental import pallas as pl
from jax.experimental.pallas import tpu as pltpu
from jax.sharding import PartitionSpec as P

CAP = 2
MESH = pl.DeviceIdType.MESH


def exchange_kernel(
    atoms, auxes, h_ref, fit_ref, out_ref,
    hall, hx, g, epart, cbuf, ybuf,
    local_sem, sx, sz0, sz, rh, sa, ra, sc, rc, sy, ry,
):
    planes, ys = atoms // 2, auxes // 2
    aux_here, rows, occ = h_ref.shape
    me = lax.axis_index("atom")
    ax = lax.axis_index("aux")
    hi, lo = me // 2, me % 2
    y, c = ax // 2, ax % 2
    partner = {"atom": hi * 2 + 1 - lo, "aux": ax}
    peer = {"atom": me, "aux": y * 2 + 1 - c}

    barrier = pltpu.get_barrier_semaphore()

    def greet(device):
        pl.semaphore_signal(barrier, inc=1, device_id=device, device_id_type=MESH)

    greet(partner)
    greet(peer)
    for d in range(1, ys):
        greet({"atom": me, "aux": ((y + d) % ys) * 2 + c})

    @pl.when(hi > 0)
    def _():
        greet({"atom": me - 2, "aux": ax})

    @pl.when(hi < planes - 1)
    def _():
        greet({"atom": me + 2, "aux": ax})

    before = jnp.minimum(hi, 1)
    behind = jnp.minimum(planes - 1 - hi, 1)
    pl.semaphore_wait(barrier, 1 + ys + before + behind)

    def remote(src, dst, send, recv, device):
        return pltpu.make_async_remote_copy(
            src_ref=src, dst_ref=dst, send_sem=send, recv_sem=recv,
            device_id=device, device_id_type=MESH,
        )

    def to_partner(k, atom, src):
        return remote(src, hall.at[atom], sx.at[k], rh.at[atom], partner)

    def along(atom, src, sem, step):
        return remote(src, hall.at[atom], sem, rh.at[atom], {"atom": me + 2 * step, "aux": ax})

    left_ok, right_ok = hi > 0, hi < planes - 1

    @pl.when(left_ok)
    def _():
        along(me, h_ref, sz0.at[0], -1).start()

    @pl.when(right_ok)
    def _():
        along(me, h_ref, sz0.at[1], 1).start()

    to_partner(0, me, h_ref).start()
    for d in range(1, ys):
        remote(h_ref, hx.at[ax], sa.at[d], ra.at[ax], {"atom": me, "aux": ((y + d) % ys) * 2 + c}).start()
    remote(h_ref, hx.at[ax], sa.at[0], ra.at[ax], peer).start()
    own = pltpu.make_async_copy(h_ref, hall.at[me], local_sem.at[0])
    own.start()
    own_aux = pltpu.make_async_copy(h_ref, hx.at[ax], local_sem.at[1])
    own_aux.start()

    def plane_of(k):
        half = (k + 1) // 2
        return hi + half * (1 - 2 * (k % 2))

    def valid(k):
        p = plane_of(k)
        return (p >= 0) & (p < planes) & (k < 2 * planes - 1)

    def forward_ok(k):
        target = hi - (1 - 2 * (k % 2))
        return valid(k) & (target >= 0) & (target < planes)

    def wait_block(atom):
        remote(h_ref, hall.at[atom], sx.at[0], rh.at[atom], partner).wait_recv()

    def relay(k):
        @pl.when(valid(k))
        def _():
            atom = plane_of(k) * 2 + lo
            wait_block(atom)

            @pl.when(forward_ok(k))
            def _():
                along(atom, hall.at[atom], sz.at[k], -(1 - 2 * (k % 2))).start()

            to_partner(k, atom, hall.at[atom]).start()

    relay(1)
    relay(2)

    for d in range(1, ys):
        src = ((y + d) % ys) * 2 + c
        remote(h_ref, hx.at[src], sa.at[0], ra.at[src], peer).wait_recv()
        remote(hx.at[src], hx.at[src], sa.at[ys - 1 + d], ra.at[src], peer).start()
    for d in range(ys):
        src = ((y + d) % ys) * 2 + 1 - c
        remote(h_ref, hx.at[src], sa.at[0], ra.at[src], peer).wait_recv()
    own_aux.wait()
    own.wait()

    piece = 32

    @pl.loop(0, rows // piece)
    def _(j):
        at = pl.ds(pl.multiple_of(j * piece, piece), piece)
        sums = [jnp.zeros((piece, occ), jnp.float32) for _ in range(aux_here)]
        for p in range(aux_here * auxes):
            block = hx[p // aux_here, p % aux_here, at, :].astype(jnp.float32)
            for q in range(aux_here):
                sums[q] = sums[q] + fit_ref[q, p] * block
        for q in range(aux_here):
            g[at, q * occ:(q + 1) * occ] = sums[q].astype(jnp.bfloat16)

    width = 256

    def product(k):
        p = plane_of(k)

        @pl.when(k > 0)
        def _():
            wait_block(p * 2 + 1 - lo)

        @pl.when(k == 0)
        def _():
            wait_block(hi * 2 + 1 - lo)

        for half in range(2):
            @pl.loop(0, rows // width)
            def _(j):
                at = pl.ds(pl.multiple_of(j * width, width), width)
                right = jnp.concatenate(
                    [hall[p * 2 + half, q, at, :] for q in range(aux_here)], axis=-1
                )
                part = lax.dot_general(
                    g[...], right, (((1,), (1,)), ((), ())), preferred_element_type=jnp.float32
                )
                col = pl.ds(pl.multiple_of(half * rows + j * width, width), width)
                epart[p, :, col] = part.astype(jnp.bfloat16)

        @pl.when(p % 2 != c)
        def _():
            remote(epart.at[p], cbuf.at[p // 2], sc.at[p // 2], rc.at[p // 2], peer).start()

    def join(k):
        p = plane_of(k)
        yt = p // 2

        @pl.when(p % 2 == c)
        def _():
            remote(epart.at[p], cbuf.at[yt], sc.at[yt], rc.at[yt], peer).wait_recv()

            @pl.when(yt != y)
            def _():
                @pl.loop(0, rows // 64)
                def _(j):
                    at = pl.ds(pl.multiple_of(j * 64, 64), 64)
                    total = epart[p, at, :].astype(jnp.float32) + cbuf[yt, at, :].astype(jnp.float32)
                    epart[p, at, :] = total.astype(jnp.bfloat16)

                remote(epart.at[p], ybuf.at[y], sy.at[yt], ry.at[y], {"atom": me, "aux": p}).start()

    @pl.loop(0, 2 * planes)
    def _(k):
        @pl.when(valid(k))
        def _():
            product(k)

        @pl.when(k > 0)
        def _():
            @pl.when(valid(k - 1))
            def _():
                join(k - 1)

        relay(k + 3)

    for d in range(1, ys):
        src = (y + d) % ys
        remote(epart.at[ax], ybuf.at[src], sy.at[src], ry.at[src], peer).wait_recv()

    @pl.loop(0, rows // 64)
    def _(j):
        at = pl.ds(pl.multiple_of(j * 64, 64), 64)
        total = epart[ax, at, :].astype(jnp.float32) + cbuf[y, at, :].astype(jnp.float32)
        for d in range(1, ys):
            total = total + ybuf[(y + d) % ys, at, :].astype(jnp.float32)
        out_ref[at, :] = total

    @pl.when(left_ok)
    def _():
        along(me, h_ref, sz0.at[0], -1).wait_send()

    @pl.when(right_ok)
    def _():
        along(me, h_ref, sz0.at[1], 1).wait_send()

    for k in range(2 * planes - 1):
        @pl.when(valid(k))
        def _():
            to_partner(k, me, h_ref).wait_send()

            if k > 0:
                @pl.when(forward_ok(k))
                def _():
                    along(me, h_ref, sz.at[k], -(1 - 2 * (k % 2))).wait_send()

    for d in range(2 * ys - 1):
        remote(h_ref, hx.at[ax], sa.at[d], ra.at[ax], peer).wait_send()
    for t in range(ys):
        remote(epart.at[ax], cbuf.at[t], sc.at[t], rc.at[t], peer).wait_send()
    for d in range(1, ys):
        remote(epart.at[ax], ybuf.at[y], sy.at[(y + d) % ys], ry.at[y], peer).wait_send()


def exchange_call(h, fit_rows):
    aux_here, rows, occ = h.shape
    atoms, auxes = lax.axis_size("atom"), lax.axis_size("aux")
    planes, ys = atoms // 2, auxes // 2
    columns = rows * atoms // auxes
    dma = pltpu.SemaphoreType.DMA
    return pl.pallas_call(
        functools.partial(exchange_kernel, atoms, auxes),
        out_shape=jax.ShapeDtypeStruct((rows, columns), jnp.float32),
        in_specs=[
            pl.BlockSpec(memory_space=pltpu.VMEM),
            pl.BlockSpec(memory_space=pltpu.SMEM),
        ],
        out_specs=pl.BlockSpec(memory_space=pltpu.VMEM),
        scratch_shapes=[
            pltpu.VMEM((atoms, aux_here, rows, occ), jnp.bfloat16),
            pltpu.VMEM((auxes, aux_here, rows, occ), jnp.bfloat16),
            pltpu.VMEM((rows, aux_here * occ), jnp.bfloat16),
            pltpu.VMEM((auxes, rows, columns), jnp.bfloat16),
            pltpu.VMEM((ys, rows, columns), jnp.bfloat16),
            pltpu.VMEM((ys, rows, columns), jnp.bfloat16),
            dma((2,)),
            dma((2 * planes - 1,)),
            dma((2,)),
            dma((2 * planes - 1,)),
            dma((atoms,)),
            dma((2 * ys - 1,)),
            dma((auxes,)),
            dma((ys,)),
            dma((ys,)),
            dma((ys,)),
            dma((ys,)),
        ],
        compiler_params=pltpu.CompilerParams(
            collective_id=0, has_side_effects=True, vmem_limit_bytes=60 * 1024 * 1024
        ),
    )(h, fit_rows)


def route_kernel(
    atoms, order_ref, nu_ref, three_ref, mask_ref, code_ref, own_ref, out_ref,
    orbitals, outgoing, arrived, codes, acc, summed, landed,
    local_sem, sx, sz0, sz, rh, sd, rd, sk, rk, cross_sem,
):
    planes, middle = atoms // 2, atoms // 2
    cap = code_ref.shape[1]
    per, size, occ = own_ref.shape
    aux_here = three_ref.shape[1]
    share = aux_here // 2
    me = lax.axis_index("atom")
    ax = lax.axis_index("aux")
    hi, lo = me // 2, me % 2
    side, pos = me // middle, me % middle

    def at_atom(atom):
        return {"atom": atom, "aux": ax}

    barrier = pltpu.get_barrier_semaphore()
    for d in range(1, atoms):
        pl.semaphore_signal(
            barrier, inc=1, device_id=at_atom((me + d) % atoms), device_id_type=MESH
        )
    pl.semaphore_wait(barrier, atoms - 1)

    def remote(src, dst, send, recv, device):
        return pltpu.make_async_remote_copy(
            src_ref=src, dst_ref=dst, send_sem=send, recv_sem=recv,
            device_id=device, device_id_type=MESH,
        )

    def spot(atom):
        return orbitals.at[pl.ds(atom * per, per)]

    def to_partner(k, atom, src):
        return remote(src, spot(atom), sx.at[k], rh.at[atom], at_atom(hi * 2 + 1 - lo))

    def along(atom, src, sem, step):
        return remote(src, spot(atom), sem, rh.at[atom], at_atom(me + 2 * step))

    left_ok, right_ok = hi > 0, hi < planes - 1

    @pl.when(left_ok)
    def _():
        along(me, own_ref, sz0.at[0], -1).start()

    @pl.when(right_ok)
    def _():
        along(me, own_ref, sz0.at[1], 1).start()

    to_partner(0, me, own_ref).start()
    own = pltpu.make_async_copy(own_ref, spot(me), local_sem.at[0])
    own.start()

    def plane_of(k):
        half = (k + 1) // 2
        return hi + half * (1 - 2 * (k % 2))

    def valid(k):
        p = plane_of(k)
        return (p >= 0) & (p < planes)

    def forward_ok(k):
        target = hi - (1 - 2 * (k % 2))
        return valid(k) & (target >= 0) & (target < planes)

    def wait_block(atom):
        remote(own_ref, spot(atom), sx.at[0], rh.at[atom], at_atom(hi * 2 + 1 - lo)).wait_recv()

    @pl.loop(1, 2 * planes - 1)
    def _(k):
        @pl.when(valid(k))
        def _():
            atom = plane_of(k) * 2 + lo
            wait_block(atom)

            @pl.when(forward_ok(k))
            def _():
                along(atom, spot(atom), sz.at[k], -(1 - 2 * (k % 2))).start()

            to_partner(k, atom, spot(atom)).start()

    @pl.loop(0, planes)
    def _(p):
        wait_block(p * 2 + 1 - lo)

    own.wait()

    def half_block(place, part):
        slot, nu = order_ref[place], nu_ref[place]
        right = orbitals[nu]
        left = three_ref[slot, part * share:(part + 1) * share] * mask_ref[slot][None, :, :]
        value = jnp.dot(
            left.reshape(share * size, size), right, preferred_element_type=jnp.float32
        )
        return value.reshape(share, size, occ).astype(jnp.bfloat16)

    def target_of(j):
        return (pos + j % (middle - 1) + 1) % middle

    def block(part, j, lane, device):
        return remote(
            outgoing.at[part, j], arrived.at[part, lane], sd.at[part, j], rd.at[part, lane], device
        )

    def start_sends(first, owner_side, part):
        @pl.loop(first, first + middle - 1)
        def _(j):
            q = target_of(j)
            owner = owner_side * middle + q
            lane = (first // (middle - 1)) * middle + pos

            @pl.loop(0, cap)
            def _(r):
                outgoing[part, j, r] = half_block(owner * cap + r, part)

            device = at_atom(side * middle + q)
            if part == 0:
                remote(code_ref.at[owner], codes.at[lane], sk.at[j], rk.at[lane], device).start()
            block(part, j, lane, device).start()

    def fill_own(lane, owner, sem):
        @pl.loop(0, cap)
        def _(r):
            for part in range(2):
                arrived[part, lane, r] = half_block(owner * cap + r, part)

        keep = pltpu.make_async_copy(code_ref.at[owner], codes.at[lane], sem)
        keep.start()
        keep.wait()

    start_sends(0, 1 - side, 0)
    start_sends(0, 1 - side, 1)
    fill_own(pos, (1 - side) * middle + pos, local_sem.at[1])
    start_sends(middle - 1, side, 0)
    start_sends(middle - 1, side, 1)
    fill_own(middle + pos, me, local_sem.at[2])

    def take(src, part):
        hits = [
            [codes[src, r, b] for r in range(cap)]
            for b in range(per)
        ]

        @pl.loop(0, share * (size // 64))
        def _(n):
            p, row = n // (size // 64), n % (size // 64)
            at = pl.ds(pl.multiple_of(row * 64, 64), 64)
            values = [
                arrived[part, src, r, p, at, :].astype(jnp.float32).reshape(8, 8, occ)
                for r in range(cap)
            ]
            for b in range(per):
                to = pl.ds(pl.multiple_of(b * size + row * 64, 64), 64)
                total = acc[part * share + p, to, :].reshape(8, 8, occ)
                for r in range(cap):
                    total = total + values[r] * hits[b][r][None]
                acc[part * share + p, to, :] = total.reshape(64, occ)

    def take_all(base, part):
        span = pl.ds(part * share, share)
        acc[span] = jnp.zeros((share,) + acc.shape[1:], jnp.float32)
        take(base + pos, part)

        @pl.loop(1, middle)
        def _(i):
            src = (pos + middle - i) % middle
            lane = base + src
            device = at_atom(side * middle + src)
            if part == 0:
                remote(code_ref.at[0], codes.at[lane], sk.at[0], rk.at[lane], device).wait_recv()
            block(part, 0, lane, device).wait_recv()
            take(lane, part)

    across = at_atom((1 - side) * middle + pos)
    crossings = []
    for part in range(2):
        take_all(0, part)
        span = pl.ds(part * share, share)
        summed[span] = acc[span].astype(jnp.bfloat16)
        cross = remote(
            summed.at[span], landed.at[span], cross_sem.at[part], cross_sem.at[2 + part], across
        )
        cross.start()
        crossings.append(cross)
    take_all(middle, 0)
    take_all(middle, 1)
    for part in range(2):
        crossings[part].wait_recv()
        span = pl.ds(part * share, share)
        out_ref[span] = (acc[span] + landed[span].astype(jnp.float32)).astype(jnp.bfloat16)
    for cross in crossings:
        cross.wait_send()

    @pl.when(left_ok)
    def _():
        along(me, own_ref, sz0.at[0], -1).wait_send()

    @pl.when(right_ok)
    def _():
        along(me, own_ref, sz0.at[1], 1).wait_send()

    to_partner(0, me, own_ref).wait_send()

    @pl.loop(1, 2 * planes - 1)
    def _(k):
        @pl.when(valid(k))
        def _():
            to_partner(k, me, own_ref).wait_send()

            @pl.when(forward_ok(k))
            def _():
                along(me, own_ref, sz.at[k], -(1 - 2 * (k % 2))).wait_send()

    @pl.loop(0, 2 * middle - 2)
    def _(j):
        device = at_atom(side * middle + target_of(j))
        block(0, j, 0, device).wait_send()
        block(1, j, 0, device).wait_send()
        remote(code_ref.at[0], codes.at[0], sk.at[j], rk.at[0], device).wait_send()


def route_call(order, nu, three_index, mask, codes, coefficients):
    aux_here, size = three_index.shape[1], three_index.shape[2]
    rows, occ = coefficients.shape
    per = rows // size
    atoms = lax.axis_size("atom")
    planes = atoms // 2
    dma = pltpu.SemaphoreType.DMA
    smem = pl.BlockSpec(memory_space=pltpu.SMEM)
    vmem = pl.BlockSpec(memory_space=pltpu.VMEM)
    return pl.pallas_call(
        functools.partial(route_kernel, atoms),
        out_shape=jax.ShapeDtypeStruct((aux_here, rows, occ), jnp.bfloat16),
        in_specs=[smem, smem, vmem, vmem, vmem, vmem],
        out_specs=vmem,
        scratch_shapes=[
            pltpu.VMEM((atoms * per, size, occ), jnp.bfloat16),
            pltpu.VMEM((2, atoms - 2, CAP, aux_here // 2, size, occ), jnp.bfloat16),
            pltpu.VMEM((2, atoms, CAP, aux_here // 2, size, occ), jnp.bfloat16),
            pltpu.VMEM((atoms, CAP, per, 8, 128), jnp.float32),
            pltpu.VMEM((aux_here, rows, occ), jnp.float32),
            pltpu.VMEM((aux_here, rows, occ), jnp.bfloat16),
            pltpu.VMEM((aux_here, rows, occ), jnp.bfloat16),
            dma((3,)),
            dma((2 * planes - 1,)),
            dma((2,)),
            dma((2 * planes - 1,)),
            dma((atoms,)),
            dma((2, atoms - 2)),
            dma((2, atoms)),
            dma((atoms - 2,)),
            dma((atoms,)),
            dma((4,)),
        ],
        compiler_params=pltpu.CompilerParams(
            collective_id=1, has_side_effects=True, vmem_limit_bytes=60 * 1024 * 1024
        ),
    )(order, nu, three_index, mask, codes, coefficients.reshape(per, size, occ))


def per_device(
    three_index, pair_mask, pair_owner, pair_sub, pair_nu, live_count, coefficients, fit_matrix
):
    slot_count, aux_here, block_size, _ = three_index.shape
    rows_here, occupied = coefficients.shape
    atom_count = lax.axis_size("atom")
    aux_total = fit_matrix.shape[1]
    shell_size = block_size // pair_mask.shape[1]
    expanded = jnp.repeat(jnp.repeat(pair_mask, shell_size, 1), shell_size, 2).astype(jnp.bfloat16)
    owners = pair_owner[:, 0]
    owner_hits = (owners[:, None] == jnp.arange(atom_count)[None, :]).astype(jnp.int32)
    rank_within = jnp.sum(jnp.cumsum(owner_hits, 0) * owner_hits, 1) - 1
    placement = owners * CAP + rank_within
    routing = (jnp.arange(atom_count * CAP)[:, None] == placement[None, :]).astype(jnp.int32)
    slots = jnp.arange(slot_count, dtype=jnp.int32)

    def placed(values):
        return jnp.sum(routing * values[None, :], 1)

    live_codes = placed(jnp.where(slots < live_count[0], pair_sub + 1, 0))
    blocks = jnp.arange(rows_here // block_size)
    hits = (live_codes[:, None] == blocks[None, :] + 1).astype(jnp.float32)
    hits = hits.reshape(atom_count, CAP, blocks.shape[0], 1, 1)
    local_rows = route_call(
        placed(slots),
        placed(pair_nu),
        three_index,
        expanded,
        jnp.broadcast_to(hits, hits.shape[:3] + (8, 128)),
        coefficients,
    )
    total = exchange_call(local_rows, fit_matrix.astype(jnp.float32))
    return total * (aux_total * occupied) ** (-0.5)


def solution(mesh):
    in_specs = (
        P("atom", "aux", None, None),
        P("atom", None, None),
        P("atom", None),
        P("atom"),
        P("atom"),
        P("atom"),
        P("atom", None),
        P("aux", None),
    )
    out_specs = P("atom", "aux")
    return jax.shard_map(
        per_device, mesh=mesh, in_specs=in_specs, out_specs=out_specs, check_vma=False
    )
```

```python
import functools

import jax
import jax.numpy as jnp
from jax import lax
from jax.experimental import pallas as pl
from jax.experimental.pallas import tpu as pltpu
from jax.sharding import PartitionSpec as P

CAP = 2
MESH = pl.DeviceIdType.MESH


def exchange_kernel(
    atoms, auxes, h_ref, fit_ref, out_ref,
    hall, hx, g, epart, cbuf, ybuf,
    local_sem, sx, sz0, sz, rh, sa, ra, sc, rc, sy, ry,
):
    planes, ys = atoms // 2, auxes // 2
    aux_here, rows, occ = h_ref.shape
    me = lax.axis_index("atom")
    ax = lax.axis_index("aux")
    hi, lo = me // 2, me % 2
    y, c = ax // 2, ax % 2
    partner = {"atom": hi * 2 + 1 - lo, "aux": ax}
    peer = {"atom": me, "aux": y * 2 + 1 - c}

    barrier = pltpu.get_barrier_semaphore()

    def greet(device):
        pl.semaphore_signal(barrier, inc=1, device_id=device, device_id_type=MESH)

    greet(partner)
    greet(peer)
    for d in range(1, ys):
        greet({"atom": me, "aux": ((y + d) % ys) * 2 + c})

    @pl.when(hi > 0)
    def _():
        greet({"atom": me - 2, "aux": ax})

    @pl.when(hi < planes - 1)
    def _():
        greet({"atom": me + 2, "aux": ax})

    before = jnp.minimum(hi, 1)
    behind = jnp.minimum(planes - 1 - hi, 1)
    pl.semaphore_wait(barrier, 1 + ys + before + behind)

    def remote(src, dst, send, recv, device):
        return pltpu.make_async_remote_copy(
            src_ref=src, dst_ref=dst, send_sem=send, recv_sem=recv,
            device_id=device, device_id_type=MESH,
        )

    def to_partner(k, atom, src):
        return remote(src, hall.at[atom], sx.at[k], rh.at[atom], partner)

    def along(atom, src, sem, step):
        return remote(src, hall.at[atom], sem, rh.at[atom], {"atom": me + 2 * step, "aux": ax})

    left_ok, right_ok = hi > 0, hi < planes - 1

    @pl.when(left_ok)
    def _():
        along(me, h_ref, sz0.at[0], -1).start()

    @pl.when(right_ok)
    def _():
        along(me, h_ref, sz0.at[1], 1).start()

    to_partner(0, me, h_ref).start()
    for d in range(1, ys):
        remote(h_ref, hx.at[ax], sa.at[d], ra.at[ax], {"atom": me, "aux": ((y + d) % ys) * 2 + c}).start()
    remote(h_ref, hx.at[ax], sa.at[0], ra.at[ax], peer).start()
    own = pltpu.make_async_copy(h_ref, hall.at[me], local_sem.at[0])
    own.start()
    own_aux = pltpu.make_async_copy(h_ref, hx.at[ax], local_sem.at[1])
    own_aux.start()

    def plane_of(k):
        half = (k + 1) // 2
        return hi + half * (1 - 2 * (k % 2))

    def valid(k):
        p = plane_of(k)
        return (p >= 0) & (p < planes) & (k < 2 * planes - 1)

    def forward_ok(k):
        target = hi - (1 - 2 * (k % 2))
        return valid(k) & (target >= 0) & (target < planes)

    def wait_block(atom):
        remote(h_ref, hall.at[atom], sx.at[0], rh.at[atom], partner).wait_recv()

    def relay(k):
        @pl.when(valid(k))
        def _():
            atom = plane_of(k) * 2 + lo
            wait_block(atom)

            @pl.when(forward_ok(k))
            def _():
                along(atom, hall.at[atom], sz.at[k], -(1 - 2 * (k % 2))).start()

            to_partner(k, atom, hall.at[atom]).start()

    relay(1)
    relay(2)

    for d in range(1, ys):
        src = ((y + d) % ys) * 2 + c
        remote(h_ref, hx.at[src], sa.at[0], ra.at[src], peer).wait_recv()
        remote(hx.at[src], hx.at[src], sa.at[ys - 1 + d], ra.at[src], peer).start()
    for d in range(ys):
        src = ((y + d) % ys) * 2 + 1 - c
        remote(h_ref, hx.at[src], sa.at[0], ra.at[src], peer).wait_recv()
    own_aux.wait()
    own.wait()

    piece = 32

    @pl.loop(0, rows // piece)
    def _(j):
        at = pl.ds(pl.multiple_of(j * piece, piece), piece)
        sums = [jnp.zeros((piece, occ), jnp.float32) for _ in range(aux_here)]
        for p in range(aux_here * auxes):
            block = hx[p // aux_here, p % aux_here, at, :].astype(jnp.float32)
            for q in range(aux_here):
                sums[q] = sums[q] + fit_ref[q, p] * block
        for q in range(aux_here):
            g[at, q * occ:(q + 1) * occ] = sums[q].astype(jnp.bfloat16)

    width = 256

    def product(k):
        p = plane_of(k)

        @pl.when(k > 0)
        def _():
            wait_block(p * 2 + 1 - lo)

        @pl.when(k == 0)
        def _():
            wait_block(hi * 2 + 1 - lo)

        for half in range(2):
            @pl.loop(0, rows // width)
            def _(j):
                at = pl.ds(pl.multiple_of(j * width, width), width)
                right = jnp.concatenate(
                    [hall[p * 2 + half, q, at, :] for q in range(aux_here)], axis=-1
                )
                part = lax.dot_general(
                    g[...], right, (((1,), (1,)), ((), ())), preferred_element_type=jnp.float32
                )
                col = pl.ds(pl.multiple_of(half * rows + j * width, width), width)
                epart[p, :, col] = part.astype(jnp.bfloat16)

        @pl.when(p % 2 != c)
        def _():
            remote(epart.at[p], cbuf.at[p // 2], sc.at[p // 2], rc.at[p // 2], peer).start()

    def join(k):
        p = plane_of(k)
        yt = p // 2

        @pl.when(p % 2 == c)
        def _():
            remote(epart.at[p], cbuf.at[yt], sc.at[yt], rc.at[yt], peer).wait_recv()

            @pl.when(yt != y)
            def _():
                @pl.loop(0, rows // 64)
                def _(j):
                    at = pl.ds(pl.multiple_of(j * 64, 64), 64)
                    total = epart[p, at, :].astype(jnp.float32) + cbuf[yt, at, :].astype(jnp.float32)
                    epart[p, at, :] = total.astype(jnp.bfloat16)

                remote(epart.at[p], ybuf.at[y], sy.at[yt], ry.at[y], {"atom": me, "aux": p}).start()

    @pl.loop(0, 2 * planes)
    def _(k):
        @pl.when(valid(k))
        def _():
            product(k)

        @pl.when(k > 0)
        def _():
            @pl.when(valid(k - 1))
            def _():
                join(k - 1)

        relay(k + 3)

    for d in range(1, ys):
        src = (y + d) % ys
        remote(epart.at[ax], ybuf.at[src], sy.at[src], ry.at[src], peer).wait_recv()

    @pl.loop(0, rows // 64)
    def _(j):
        at = pl.ds(pl.multiple_of(j * 64, 64), 64)
        total = epart[ax, at, :].astype(jnp.float32) + cbuf[y, at, :].astype(jnp.float32)
        for d in range(1, ys):
            total = total + ybuf[(y + d) % ys, at, :].astype(jnp.float32)
        out_ref[at, :] = total

    @pl.when(left_ok)
    def _():
        along(me, h_ref, sz0.at[0], -1).wait_send()

    @pl.when(right_ok)
    def _():
        along(me, h_ref, sz0.at[1], 1).wait_send()

    for k in range(2 * planes - 1):
        @pl.when(valid(k))
        def _():
            to_partner(k, me, h_ref).wait_send()

            if k > 0:
                @pl.when(forward_ok(k))
                def _():
                    along(me, h_ref, sz.at[k], -(1 - 2 * (k % 2))).wait_send()

    for d in range(2 * ys - 1):
        remote(h_ref, hx.at[ax], sa.at[d], ra.at[ax], peer).wait_send()
    for t in range(ys):
        remote(epart.at[ax], cbuf.at[t], sc.at[t], rc.at[t], peer).wait_send()
    for d in range(1, ys):
        remote(epart.at[ax], ybuf.at[y], sy.at[(y + d) % ys], ry.at[y], peer).wait_send()


def exchange_call(h, fit_rows):
    aux_here, rows, occ = h.shape
    atoms, auxes = lax.axis_size("atom"), lax.axis_size("aux")
    planes, ys = atoms // 2, auxes // 2
    columns = rows * atoms // auxes
    dma = pltpu.SemaphoreType.DMA
    return pl.pallas_call(
        functools.partial(exchange_kernel, atoms, auxes),
        out_shape=jax.ShapeDtypeStruct((rows, columns), jnp.float32),
        in_specs=[
            pl.BlockSpec(memory_space=pltpu.VMEM),
            pl.BlockSpec(memory_space=pltpu.SMEM),
        ],
        out_specs=pl.BlockSpec(memory_space=pltpu.VMEM),
        scratch_shapes=[
            pltpu.VMEM((atoms, aux_here, rows, occ), jnp.bfloat16),
            pltpu.VMEM((auxes, aux_here, rows, occ), jnp.bfloat16),
            pltpu.VMEM((rows, aux_here * occ), jnp.bfloat16),
            pltpu.VMEM((auxes, rows, columns), jnp.bfloat16),
            pltpu.VMEM((ys, rows, columns), jnp.bfloat16),
            pltpu.VMEM((ys, rows, columns), jnp.bfloat16),
            dma((2,)),
            dma((2 * planes - 1,)),
            dma((2,)),
            dma((2 * planes - 1,)),
            dma((atoms,)),
            dma((2 * ys - 1,)),
            dma((auxes,)),
            dma((ys,)),
            dma((ys,)),
            dma((ys,)),
            dma((ys,)),
        ],
        compiler_params=pltpu.CompilerParams(
            collective_id=0, has_side_effects=True, vmem_limit_bytes=60 * 1024 * 1024
        ),
    )(h, fit_rows)


def route_kernel(
    atoms, order_ref, nu_ref, three_ref, mask_ref, code_ref, own_ref, out_ref,
    orbitals, outgoing, arrived, codes, acc, summed, landed,
    local_sem, sx, sz0, sz, rh, sd, rd, sk, rk, cross_sem,
):
    planes, middle = atoms // 2, atoms // 2
    cap = code_ref.shape[1]
    per, size, occ = own_ref.shape
    aux_here = three_ref.shape[1]
    share = aux_here // 2
    me = lax.axis_index("atom")
    ax = lax.axis_index("aux")
    hi, lo = me // 2, me % 2
    side, pos = me // middle, me % middle

    def at_atom(atom):
        return {"atom": atom, "aux": ax}

    barrier = pltpu.get_barrier_semaphore()
    for d in range(1, atoms):
        pl.semaphore_signal(
            barrier, inc=1, device_id=at_atom((me + d) % atoms), device_id_type=MESH
        )
    pl.semaphore_wait(barrier, atoms - 1)

    def remote(src, dst, send, recv, device):
        return pltpu.make_async_remote_copy(
            src_ref=src, dst_ref=dst, send_sem=send, recv_sem=recv,
            device_id=device, device_id_type=MESH,
        )

    def spot(atom):
        return orbitals.at[pl.ds(atom * per, per)]

    def to_partner(k, atom, src):
        return remote(src, spot(atom), sx.at[k], rh.at[atom], at_atom(hi * 2 + 1 - lo))

    def along(atom, src, sem, step):
        return remote(src, spot(atom), sem, rh.at[atom], at_atom(me + 2 * step))

    left_ok, right_ok = hi > 0, hi < planes - 1

    @pl.when(left_ok)
    def _():
        along(me, own_ref, sz0.at[0], -1).start()

    @pl.when(right_ok)
    def _():
        along(me, own_ref, sz0.at[1], 1).start()

    to_partner(0, me, own_ref).start()
    own = pltpu.make_async_copy(own_ref, spot(me), local_sem.at[0])
    own.start()

    def plane_of(k):
        half = (k + 1) // 2
        return hi + half * (1 - 2 * (k % 2))

    def valid(k):
        p = plane_of(k)
        return (p >= 0) & (p < planes)

    def forward_ok(k):
        target = hi - (1 - 2 * (k % 2))
        return valid(k) & (target >= 0) & (target < planes)

    def wait_block(atom):
        remote(own_ref, spot(atom), sx.at[0], rh.at[atom], at_atom(hi * 2 + 1 - lo)).wait_recv()

    @pl.loop(1, 2 * planes - 1)
    def _(k):
        @pl.when(valid(k))
        def _():
            atom = plane_of(k) * 2 + lo
            wait_block(atom)

            @pl.when(forward_ok(k))
            def _():
                along(atom, spot(atom), sz.at[k], -(1 - 2 * (k % 2))).start()

            to_partner(k, atom, spot(atom)).start()

    @pl.loop(0, planes)
    def _(p):
        wait_block(p * 2 + 1 - lo)

    own.wait()

    def half_block(place, part):
        slot, nu = order_ref[place], nu_ref[place]
        right = orbitals[nu]
        left = three_ref[slot, part * share:(part + 1) * share] * mask_ref[slot][None, :, :]
        value = jnp.dot(
            left.reshape(share * size, size), right, preferred_element_type=jnp.float32
        )
        return value.reshape(share, size, occ).astype(jnp.bfloat16)

    def target_of(j):
        return (pos + j % (middle - 1) + 1) % middle

    def block(part, j, lane, device):
        return remote(
            outgoing.at[part, j], arrived.at[part, lane], sd.at[part, j], rd.at[part, lane], device
        )

    def start_sends(first, owner_side, part):
        @pl.loop(first, first + middle - 1)
        def _(j):
            q = target_of(j)
            owner = owner_side * middle + q
            lane = (first // (middle - 1)) * middle + pos

            @pl.loop(0, cap)
            def _(r):
                outgoing[part, j, r] = half_block(owner * cap + r, part)

            device = at_atom(side * middle + q)
            if part == 0:
                remote(code_ref.at[owner], codes.at[lane], sk.at[j], rk.at[lane], device).start()
            block(part, j, lane, device).start()

    def fill_own(lane, owner, sem):
        @pl.loop(0, cap)
        def _(r):
            for part in range(2):
                arrived[part, lane, r] = half_block(owner * cap + r, part)

        keep = pltpu.make_async_copy(code_ref.at[owner], codes.at[lane], sem)
        keep.start()
        keep.wait()

    start_sends(0, 1 - side, 0)
    start_sends(0, 1 - side, 1)
    fill_own(pos, (1 - side) * middle + pos, local_sem.at[1])
    start_sends(middle - 1, side, 0)
    start_sends(middle - 1, side, 1)

    def take(src, part):
        hits = [
            [codes[src, r, b] for r in range(cap)]
            for b in range(per)
        ]

        @pl.loop(0, share * (size // 64))
        def _(n):
            p, row = n // (size // 64), n % (size // 64)
            at = pl.ds(pl.multiple_of(row * 64, 64), 64)
            values = [
                arrived[part, src, r, p, at, :].astype(jnp.float32).reshape(8, 8, occ)
                for r in range(cap)
            ]
            for b in range(per):
                to = pl.ds(pl.multiple_of(b * size + row * 64, 64), 64)
                total = acc[part * share + p, to, :].reshape(8, 8, occ)
                for r in range(cap):
                    total = total + values[r] * hits[b][r][None]
                acc[part * share + p, to, :] = total.reshape(64, occ)

    def take_all(base, part):
        span = pl.ds(part * share, share)
        acc[span] = jnp.zeros((share,) + acc.shape[1:], jnp.float32)
        take(base + pos, part)

        @pl.loop(1, middle)
        def _(i):
            src = (pos + middle - i) % middle
            lane = base + src
            device = at_atom(side * middle + src)
            if part == 0:
                remote(code_ref.at[0], codes.at[lane], sk.at[0], rk.at[lane], device).wait_recv()
            block(part, 0, lane, device).wait_recv()
            take(lane, part)

    across = at_atom((1 - side) * middle + pos)
    crossings = []
    for part in range(2):
        take_all(0, part)
        span = pl.ds(part * share, share)
        summed[span] = acc[span].astype(jnp.bfloat16)
        cross = remote(
            summed.at[span], landed.at[span], cross_sem.at[part], cross_sem.at[2 + part], across
        )
        cross.start()
        crossings.append(cross)
    fill_own(middle + pos, me, local_sem.at[2])
    take_all(middle, 0)
    take_all(middle, 1)
    for part in range(2):
        crossings[part].wait_recv()
        span = pl.ds(part * share, share)
        out_ref[span] = (acc[span] + landed[span].astype(jnp.float32)).astype(jnp.bfloat16)
    for cross in crossings:
        cross.wait_send()

    @pl.when(left_ok)
    def _():
        along(me, own_ref, sz0.at[0], -1).wait_send()

    @pl.when(right_ok)
    def _():
        along(me, own_ref, sz0.at[1], 1).wait_send()

    to_partner(0, me, own_ref).wait_send()

    @pl.loop(1, 2 * planes - 1)
    def _(k):
        @pl.when(valid(k))
        def _():
            to_partner(k, me, own_ref).wait_send()

            @pl.when(forward_ok(k))
            def _():
                along(me, own_ref, sz.at[k], -(1 - 2 * (k % 2))).wait_send()

    @pl.loop(0, 2 * middle - 2)
    def _(j):
        device = at_atom(side * middle + target_of(j))
        block(0, j, 0, device).wait_send()
        block(1, j, 0, device).wait_send()
        remote(code_ref.at[0], codes.at[0], sk.at[j], rk.at[0], device).wait_send()


def route_call(order, nu, three_index, mask, codes, coefficients):
    aux_here, size = three_index.shape[1], three_index.shape[2]
    rows, occ = coefficients.shape
    per = rows // size
    atoms = lax.axis_size("atom")
    planes = atoms // 2
    dma = pltpu.SemaphoreType.DMA
    smem = pl.BlockSpec(memory_space=pltpu.SMEM)
    vmem = pl.BlockSpec(memory_space=pltpu.VMEM)
    return pl.pallas_call(
        functools.partial(route_kernel, atoms),
        out_shape=jax.ShapeDtypeStruct((aux_here, rows, occ), jnp.bfloat16),
        in_specs=[smem, smem, vmem, vmem, vmem, vmem],
        out_specs=vmem,
        scratch_shapes=[
            pltpu.VMEM((atoms * per, size, occ), jnp.bfloat16),
            pltpu.VMEM((2, atoms - 2, CAP, aux_here // 2, size, occ), jnp.bfloat16),
            pltpu.VMEM((2, atoms, CAP, aux_here // 2, size, occ), jnp.bfloat16),
            pltpu.VMEM((atoms, CAP, per, 8, 128), jnp.float32),
            pltpu.VMEM((aux_here, rows, occ), jnp.float32),
            pltpu.VMEM((aux_here, rows, occ), jnp.bfloat16),
            pltpu.VMEM((aux_here, rows, occ), jnp.bfloat16),
            dma((3,)),
            dma((2 * planes - 1,)),
            dma((2,)),
            dma((2 * planes - 1,)),
            dma((atoms,)),
            dma((2, atoms - 2)),
            dma((2, atoms)),
            dma((atoms - 2,)),
            dma((atoms,)),
            dma((4,)),
        ],
        compiler_params=pltpu.CompilerParams(
            collective_id=1, has_side_effects=True, vmem_limit_bytes=60 * 1024 * 1024
        ),
    )(order, nu, three_index, mask, codes, coefficients.reshape(per, size, occ))


def per_device(
    three_index, pair_mask, pair_owner, pair_sub, pair_nu, live_count, coefficients, fit_matrix
):
    slot_count, aux_here, block_size, _ = three_index.shape
    rows_here, occupied = coefficients.shape
    atom_count = lax.axis_size("atom")
    aux_total = fit_matrix.shape[1]
    shell_size = block_size // pair_mask.shape[1]
    expanded = jnp.repeat(jnp.repeat(pair_mask, shell_size, 1), shell_size, 2).astype(jnp.bfloat16)
    owners = pair_owner[:, 0]
    owner_hits = (owners[:, None] == jnp.arange(atom_count)[None, :]).astype(jnp.int32)
    rank_within = jnp.sum(jnp.cumsum(owner_hits, 0) * owner_hits, 1) - 1
    placement = owners * CAP + rank_within
    routing = (jnp.arange(atom_count * CAP)[:, None] == placement[None, :]).astype(jnp.int32)
    slots = jnp.arange(slot_count, dtype=jnp.int32)

    def placed(values):
        return jnp.sum(routing * values[None, :], 1)

    live_codes = placed(jnp.where(slots < live_count[0], pair_sub + 1, 0))
    blocks = jnp.arange(rows_here // block_size)
    hits = (live_codes[:, None] == blocks[None, :] + 1).astype(jnp.float32)
    hits = hits.reshape(atom_count, CAP, blocks.shape[0], 1, 1)
    local_rows = route_call(
        placed(slots),
        placed(pair_nu),
        three_index,
        expanded,
        jnp.broadcast_to(hits, hits.shape[:3] + (8, 128)),
        coefficients,
    )
    total = exchange_call(local_rows, fit_matrix.astype(jnp.float32))
    return total * (aux_total * occupied) ** (-0.5)


def solution(mesh):
    in_specs = (
        P("atom", "aux", None, None),
        P("atom", None, None),
        P("atom", None),
        P("atom"),
        P("atom"),
        P("atom"),
        P("atom", None),
        P("aux", None),
    )
    out_specs = P("atom", "aux")
    return jax.shard_map(
        per_device, mesh=mesh, in_specs=in_specs, out_specs=out_specs, check_vma=False
    )
```
